512 devices in a mesh: kq: 128 (over y, z, core), band: 4 (over x).
Axes of the slice: x: 4, y: 8, z: 8, core: 2. Of those that a mesh axis runs over, the one named last changes fastest.
Arguments:
- band_functions: bfloat16 [128, 2, 16, 4096], P('kq', None, 'band'), may hold values from -6 to 6
- screening: bfloat16 [128, 2, 512, 512], P('kq'), may hold values from -0.1875 to 0.1875
- exciton: bfloat16 [128, 2, 64], P('kq'), may hold values from -6 to 6
- pair_list: int32 [1024, 2], P('kq'), may hold values from 0 to 127, as said below
Outputs:
- kernel_action: float32 [128, 2, 64], P('kq', None, 'band')
The draws below stay inside these ranges and needn't reach their ends.
Inputs may be any that keep to these rules, and one draw needn't show every extreme that they name: `pair_list`: rows d * 8 to d * 8 + 7 are the pairs of momentum transfer d: their second point is (first point - d) mod 128. Row d * 8 + s has second point c_s, the same for every d, and first point (d + c_s) mod 128; the c_s are distinct. Every k-point is the first point of exactly 8 pairs.
All inputs are finite; a program needn't handle non-finite values.
Results may differ from the reference program's by a relative error of at most 0.0074.
Values may be sent and summed in bfloat16 or wider, within the bound.
No kernel may reach another device: no remote copies, remote signals or barrier semaphores. Data moves between devices by JAX's collectives and lax.ppermute only.
A program may use at most 64 MiB of HBM per device.

```python
import math
import jax
import jax.numpy as jnp
from jax import lax

NV = 8
NC = 8
GRID_SIDE = 16
GSIDE = 8
PD = 8
NB = 16
GRID = 4096
NG = 512
NK = 128
PAIRS = 1024
N_KQ = 128
N_BAND = 4


def draw_pair_list(key, part):
    shuffled = jax.random.permutation(jax.random.fold_in(key, 17), jnp.arange(NK, dtype=jnp.int32))
    offsets = shuffled[:PD].astype(jnp.int32)
    owner_index = jnp.arange(NK, dtype=jnp.int32)[:, None]
    first_point = (owner_index + offsets[None, :]) % NK
    second_point = jnp.broadcast_to(offsets[None, :], (NK, PD)).astype(jnp.int32)
    return jnp.stack([first_point, second_point], axis=-1).reshape(NK * PD, 2).astype(jnp.int32)


def block_levels(stream_key, shape, cuts, low, top_value):
    loudness, own = 1.0, jax.random.fold_in(stream_key, 6)
    for position, blocks in cuts:
        steps = jnp.exp(jax.random.uniform(jax.random.fold_in(own, position), (blocks,), jnp.float32, low / len(cuts), top_value / len(cuts)))
        loudness = loudness * jnp.repeat(steps, shape[position] // blocks).reshape([-1 if axis == position else 1 for axis in range(len(shape))])
    return loudness


def noise(own_key, shape, spread, limit, shards=(), kind=jnp.bfloat16):
    loudness = block_levels(own_key, shape, shards, -0.22, 0.18) if shards else 1.0
    values = jax.random.normal(own_key, shape, jnp.float32) * spread * loudness
    return jnp.minimum(jnp.maximum(values, -limit), limit).astype(kind)


def setup_inputs(seed: int = 0) -> dict:
    seeds = jax.random.split(jax.random.key(seed), 5)
    band_functions = noise(seeds[0], (NK, 2, NB, GRID), 1.0, 6.0, ((0, 128), (2, 4)))
    screening = noise(seeds[1], (NK, 2, NG, NG), (2 * NG) ** -0.5, 0.1875, ((0, 128),))
    exciton = noise(seeds[2], (NK, 2, NV * NC), 1.0, 6.0, ((0, 128),))
    pair_list = draw_pair_list(jax.random.fold_in(seeds[4], 71), 0)
    return {"band_functions": band_functions, "screening": screening, "exciton": exciton, "pair_list": pair_list}


def phase_tables(first_cell, cell_count, grid_side, plane_side, planes):
    grid_cells = first_cell + jnp.arange(cell_count, dtype=jnp.int32)
    cell_x = grid_cells // (grid_side * grid_side)
    cell_y = grid_cells // grid_side % grid_side
    cell_z = grid_cells % grid_side
    wave_index = jnp.arange(planes, dtype=jnp.int32)
    half_side = plane_side // 2
    wave_x = wave_index // (plane_side * plane_side) - half_side
    wave_y = wave_index // plane_side % plane_side - half_side
    wave_z = wave_index % plane_side - half_side
    phase_index = (cell_x[:, None] * wave_x[None, :] + cell_y[:, None] * wave_y[None, :] + cell_z[:, None] * wave_z[None, :]) % grid_side
    angles = phase_index.astype(jnp.float32) * (2.0 * math.pi / grid_side)
    return (jnp.cos(angles).astype(jnp.bfloat16), jnp.sin(angles).astype(jnp.bfloat16))

def pair_densities(left_funcs, right_funcs):
    left_re = left_funcs[:, 0, :, None, :]
    left_im = left_funcs[:, 1, :, None, :]
    right_re = right_funcs[:, 0, None, :, :]
    right_im = right_funcs[:, 1, None, :, :]
    dens_re = left_re * right_re + left_im * right_im
    dens_im = left_re * right_im - left_im * right_re
    return (dens_re.astype(jnp.bfloat16), dens_im.astype(jnp.bfloat16))

def to_waves(dens_re, dens_im, cos_table, sin_table, grid_total):
    row_count = dens_re.shape[0]
    stacked = jnp.concatenate([dens_re, dens_im], axis=0)
    with_cos = jnp.dot(stacked, cos_table, preferred_element_type=jnp.float32)
    with_sin = jnp.dot(stacked, sin_table, preferred_element_type=jnp.float32)
    scale = 1.0 / math.sqrt(grid_total)
    wave_re = (with_cos[:row_count] + with_sin[row_count:]) * scale
    wave_im = (with_cos[row_count:] - with_sin[:row_count]) * scale
    return (wave_re.astype(jnp.bfloat16), wave_im.astype(jnp.bfloat16))

def reference(band_functions, screening, exciton, pair_list):
    grid_total = band_functions.shape[-1]
    planes = screening.shape[-1]
    cos_table, sin_table = phase_tables(0, grid_total, GRID_SIDE, GSIDE, planes)
    shaped_funcs = band_functions.astype(jnp.float32).reshape(NK, 2, N_BAND, 2, NV // N_BAND, grid_total)
    valence = shaped_funcs[:, :, :, 0].reshape(NK, 2, NV, grid_total)
    conduction = shaped_funcs[:, :, :, 1].reshape(NK, 2, NC, grid_total)
    amplitudes = exciton.astype(jnp.float32)
    pairs_owned = pair_list.reshape(N_KQ, PD, 2)
    highest = lax.Precision.HIGHEST

    def owner_terms(owner_args):
        owner_index, owned_pairs = owner_args
        first_point = owned_pairs[:, 0]
        second_point = owned_pairs[:, 1]
        val_re, val_im = pair_densities(valence[first_point], valence[second_point])
        cond_re, cond_im = pair_densities(conduction[first_point], conduction[second_point])
        wv_re, wv_im = to_waves(val_re.reshape(-1, grid_total), val_im.reshape(-1, grid_total), cos_table, sin_table, grid_total)
        wc_re, wc_im = to_waves(cond_re.reshape(-1, grid_total), cond_im.reshape(-1, grid_total), cos_table, sin_table, grid_total)
        weight_re = screening[owner_index, 0]
        weight_im = screening[owner_index, 1]
        scr_re = (jnp.dot(wv_re, weight_re.T, preferred_element_type=jnp.float32) - jnp.dot(wv_im, weight_im.T, preferred_element_type=jnp.float32)).astype(jnp.bfloat16)
        scr_im = (jnp.dot(wv_im, weight_re.T, preferred_element_type=jnp.float32) + jnp.dot(wv_re, weight_im.T, preferred_element_type=jnp.float32)).astype(jnp.bfloat16)
        cr = wc_re.astype(jnp.float32).reshape(PD, NC * NC, planes)
        ci = wc_im.astype(jnp.float32).reshape(PD, NC * NC, planes)
        sr = scr_re.astype(jnp.float32).reshape(PD, NV * NV, planes)
        si = scr_im.astype(jnp.float32).reshape(PD, NV * NV, planes)
        kern_re = (jnp.einsum('pag,pbg->pab', cr, sr, precision=highest) + jnp.einsum('pag,pbg->pab', ci, si, precision=highest)) / planes
        kern_im = (jnp.einsum('pag,pbg->pab', cr, si, precision=highest) - jnp.einsum('pag,pbg->pab', ci, sr, precision=highest)) / planes
        kern_re = jnp.transpose(kern_re.reshape(PD, NC, NC, NV, NV), (0, 3, 1, 4, 2)).reshape(PD, NV * NC, NV * NC)
        kern_im = jnp.transpose(kern_im.reshape(PD, NC, NC, NV, NV), (0, 3, 1, 4, 2)).reshape(PD, NV * NC, NV * NC)
        far_amps = amplitudes[second_point]
        near_amps = amplitudes[first_point]
        direct_re = jnp.einsum('pab,pb->pa', kern_re, far_amps[:, 0], precision=highest) - jnp.einsum('pab,pb->pa', kern_im, far_amps[:, 1], precision=highest)
        direct_im = jnp.einsum('pab,pb->pa', kern_re, far_amps[:, 1], precision=highest) + jnp.einsum('pab,pb->pa', kern_im, far_amps[:, 0], precision=highest)
        back_re = jnp.einsum('pab,pa->pb', kern_re, near_amps[:, 0], precision=highest) + jnp.einsum('pab,pa->pb', kern_im, near_amps[:, 1], precision=highest)
        back_im = jnp.einsum('pab,pa->pb', kern_re, near_amps[:, 1], precision=highest) - jnp.einsum('pab,pa->pb', kern_im, near_amps[:, 0], precision=highest)
        return (jnp.stack([direct_re, direct_im], axis=1), jnp.stack([back_re, back_im], axis=1))
    owners = jnp.arange(N_KQ, dtype=jnp.int32)
    direct_all, back_all = lax.map(owner_terms, (owners, pairs_owned))
    direct_all = direct_all.reshape(PAIRS, 2, NV * NC)
    back_all = back_all.reshape(PAIRS, 2, NV * NC)
    result = jnp.zeros((NK, 2, NV * NC), jnp.float32)
    result = result.at[pair_list[:, 0].astype(jnp.int32)].add(direct_all)
    result = result.at[pair_list[:, 1].astype(jnp.int32)].add(back_all)
    return result
```

```python
import functools
import math

import jax
import jax.numpy as jnp
import numpy as np
from jax import lax
from jax.experimental import pallas as pl
from jax.experimental.pallas import tpu as pltpu
from jax.sharding import PartitionSpec as P

SIDE = 16
BOX = 8
PLANE = SIDE * SIDE
HALF = BOX * BOX
NG = BOX * HALF
BLOCKS = 4
NT = (((1,), (1,)), ((), ()))


def plane_table():
    y, z = np.divmod(np.arange(PLANE), SIDE)
    gy, gz = np.divmod(np.arange(HALF), BOX)
    m = (y[:, None] * (gy - 4)[None] + z[:, None] * (gz - 4)[None]) % SIDE
    c, s = np.cos(2 * np.pi * m / SIDE), np.sin(2 * np.pi * m / SIDE)
    top = np.concatenate([c, -s, -s, -c], axis=1)
    low = np.concatenate([s, c, c, -s], axis=1)
    return np.concatenate([top, low], axis=0)


def band_of(place):
    return 2 * (place & 3) + (place >> 2)


def weighted(terms):
    total = None
    for factor, value in terms:
        if abs(factor) < 1e-9:
            continue
        if abs(abs(factor) - 1.0) < 1e-9:
            piece = value if factor > 0 else -value
        else:
            piece = value * factor
        total = piece if total is None else total + piece
    return total


def pair_body(
    ints_ref, funcs_ref, screen_ref, table_ref, amps_ref, out_ref, dens, sums, wave_re, wave_im
):
    f32, bf16 = jnp.float32, jnp.bfloat16
    points = amps_ref.shape[0]

    def densities(x, carry):
        tile = [[funcs_ref[(ri * 4 + i) * SIDE + x].astype(f32) for i in range(4)] for ri in range(2)]
        for kind in range(2):
            for s in range(2):

                def bands(ri, base):
                    low, high = tile[ri][2 * kind], tile[ri][2 * kind + 1]
                    return jnp.concatenate([low[base : base + 4], high[base : base + 4]], axis=0)

                left_re, left_im = bands(0, 4 * s)[:, None, :], bands(1, 4 * s)[:, None, :]
                right_re, right_im = bands(0, 8 + 4 * s)[None], bands(1, 8 + 4 * s)[None]
                dens_re = (left_re * right_re + left_im * right_im).reshape(64, PLANE)
                dens_im = (left_re * right_im - left_im * right_re).reshape(64, PLANE)
                row = (kind * 2 + s) * 64
                dens[x, row : row + 64, :PLANE] = dens_re.astype(bf16)
                dens[x, row : row + 64, PLANE:] = dens_im.astype(bf16)
        return carry

    lax.fori_loop(0, SIDE, densities, 0)

    def plane_sums(x, carry):
        sums[x] = jnp.dot(dens[x], table_ref[...], preferred_element_type=f32)
        return carry

    lax.fori_loop(0, SIDE, plane_sums, 0)

    scale = 1.0 / math.sqrt(SIDE**3)
    low_lanes = lax.broadcasted_iota(jnp.int32, (16, 128), 1) < HALF

    def along_x(chunk, carry):
        rows = pl.ds(pl.multiple_of(chunk * 16, 16), 16)
        out = {}
        for parity in range(2):
            sign = 1.0 if parity == 0 else -1.0
            straight, turned = [], []
            for x in range(8):
                straight.append(sums[x, rows, 0:128] + sign * sums[x + 8, rows, 0:128])
                turned.append(sums[x, rows, 128:256] + sign * sums[x + 8, rows, 128:256])
            for g in (0, 2, 4) if parity == 0 else (1, 3):
                angle = [2 * math.pi * x * g / SIDE for x in range(8)]
                even = weighted([(math.cos(a), v) for a, v in zip(angle, straight)])
                odd = weighted([(math.sin(a), v) for a, v in zip(angle, turned)])
                if odd is None:
                    out[-g] = even
                else:
                    out[g], out[-g] = even + odd, even - odd
        for pair in range(4):
            first, second = out[2 * pair - 4] * scale, out[2 * pair - 3] * scale
            re = jnp.where(low_lanes, first, pltpu.roll(second, 64, 1))
            im = jnp.where(low_lanes, pltpu.roll(first, 64, 1), second)
            wave_re[rows, pair * 128 : pair * 128 + 128] = re.astype(bf16)
            wave_im[rows, pair * 128 : pair * 128 + 128] = im.astype(bf16)
        return carry

    lax.fori_loop(0, 16, along_x, 0)

    stacked = jnp.concatenate([wave_re[0:128], wave_im[0:128]], axis=0)
    with_re = lax.dot_general(stacked, screen_ref[0], NT, preferred_element_type=f32)
    with_im = lax.dot_general(stacked, screen_ref[1], NT, preferred_element_type=f32)
    scr_re = (with_re[:128] - with_im[128:]).astype(bf16)
    scr_im = (with_re[128:] + with_im[:128]).astype(bf16)

    here = ints_ref[0]
    second_point = [ints_ref[1], ints_ref[2]]
    first_point = [(here + c) & (points - 1) for c in second_point]
    row8 = lax.broadcasted_iota(jnp.int32, (8, points), 0)
    col8 = lax.broadcasted_iota(jnp.int32, (8, points), 1)
    wanted = jnp.where(
        row8 == 0,
        first_point[0],
        jnp.where(row8 == 1, first_point[1], jnp.where(row8 == 2, second_point[0], second_point[1])),
    )
    chosen = jnp.dot(
        jnp.where(col8 == wanted, 1.0, 0.0).astype(bf16), amps_ref[...], preferred_element_type=f32
    )

    def iota(shape, axis):
        return lax.broadcasted_iota(jnp.int32, shape, axis)

    row, lane = iota((64, 128), 0), iota((64, 128), 1)
    row_hi, row_lo = band_of(row >> 3), band_of(row & 7)
    q, l = iota((128, 64), 0), iota((128, 64), 1)
    q_band = (q & 63) >> 3
    pick_hi = jnp.where(q_band == band_of(l >> 3), 1.0, 0.0).astype(bf16)
    pick_lo = jnp.where(q_band == band_of(l & 7), 1.0, 0.0).astype(bf16)

    def spread(values, row_band, pick):
        kept = jnp.where((lane & 7) == row_band, jnp.broadcast_to(values, (64, 128)), 0.0)
        re = jnp.where(lane < 64, kept, 0.0).astype(bf16)
        im = jnp.where(lane < 64, 0.0, kept).astype(bf16)
        return (
            jnp.dot(re, pick, preferred_element_type=f32),
            jnp.dot(im, pick, preferred_element_type=f32),
        )

    out_band = 2 * (lane >> 5) + ((lane >> 3) & 1)
    out_part = (lane >> 4) & 1
    out_other = lane & 7
    gather_hi = jnp.where(row_hi == out_band, 1.0, 0.0)
    gather_lo = jnp.where(row_lo == out_band, 1.0, 0.0)

    def collect(re, im, gather, row_band):
        dot = functools.partial(
            jnp.dot, precision=lax.Precision.HIGHEST, preferred_element_type=f32
        )
        both = dot(re, jnp.where(out_part == 0, gather, 0.0)) + dot(
            im, jnp.where(out_part == 1, gather, 0.0)
        )
        return jnp.sum(jnp.where(row_band == out_other, both, 0.0), axis=0, keepdims=True)

    k = iota((points, 128), 0)
    total = jnp.zeros((points, 128), f32)
    for s in range(2):
        cond, val = slice(128 + 64 * s, 192 + 64 * s), slice(64 * s, 64 * s + 64)
        cr, ci, sr, si = wave_re[cond], wave_im[cond], scr_re[val], scr_im[val]

        def nt(a, b):
            return lax.dot_general(a, b, NT, preferred_element_type=f32)

        kern_re = (nt(cr, sr) + nt(ci, si)) * (1.0 / NG)
        kern_im = (nt(cr, si) - nt(ci, sr)) * (1.0 / NG)
        far_re, far_im = spread(chosen[2 + s : 3 + s], row_lo, pick_lo)
        near_re, near_im = spread(chosen[s : s + 1], row_hi, pick_hi)
        direct = collect(
            kern_re * far_re - kern_im * far_im,
            kern_re * far_im + kern_im * far_re,
            gather_hi,
            row_hi,
        )
        back = collect(
            kern_re * near_re + kern_im * near_im,
            kern_re * near_im - kern_im * near_re,
            gather_lo,
            row_lo,
        )
        total += jnp.where(k == first_point[s], jnp.broadcast_to(direct, (points, 128)), 0.0)
        total += jnp.where(k == second_point[s], jnp.broadcast_to(back, (points, 128)), 0.0)
    out_ref[...] = total


def pair_terms(ints, funcs, screen, table, amps, interpret=False):
    points = amps.shape[0]
    vmem = pl.BlockSpec(memory_space=pltpu.VMEM)
    return pl.pallas_call(
        pair_body,
        out_shape=jax.ShapeDtypeStruct((points, 128), jnp.float32),
        in_specs=[pl.BlockSpec(memory_space=pltpu.SMEM)] + [vmem] * 4,
        out_specs=vmem,
        scratch_shapes=[
            pltpu.VMEM((SIDE, 256, 2 * PLANE), jnp.bfloat16),
            pltpu.VMEM((SIDE, 256, 4 * HALF), jnp.float32),
            pltpu.VMEM((256, NG), jnp.bfloat16),
            pltpu.VMEM((256, NG), jnp.bfloat16),
        ],
        compiler_params=pltpu.CompilerParams(vmem_limit_bytes=32 << 20),
        name="pair_terms",
        interpret=interpret,
    )(ints, funcs, screen, table, amps)


def local(band_functions, screening, exciton, pair_list):
    bf16 = jnp.bfloat16
    points = lax.axis_size("kq")
    here, block = lax.axis_index("kq"), lax.axis_index("band")
    second = lax.dynamic_slice_in_dim(pair_list[:, 1], 2 * block, 2)

    pieces = band_functions.reshape(points, 2, 128)
    amp_rows = jnp.broadcast_to(exciton.reshape(1, 1, 128), (points, 2, 128))
    held = lax.all_to_all(jnp.concatenate([pieces, amp_rows], axis=1), "kq", 0, 0, tiled=True)
    amps = held[:, 2]
    mine = held[:, :2]
    every = lax.all_to_all(
        jnp.broadcast_to(mine[None], (BLOCKS, points, 2, 128)), "band", 0, 0, tiled=True
    )

    slot = jnp.arange(16, dtype=jnp.int32)
    moved = jnp.where((slot & 4) == 0, second[0], second[1])
    owner = jnp.arange(points, dtype=jnp.int32)
    point = jnp.where(slot[None] < 8, (owner[:, None] + moved[None]) % points, moved[None])
    source = ((slot & 3)[None] * points + point).reshape(-1)
    picker = (source[:, None] == jnp.arange(BLOCKS * points, dtype=jnp.int32)[None]).astype(bf16)
    sent = jnp.dot(picker, every.reshape(BLOCKS * points, PLANE), preferred_element_type=jnp.float32)
    sent = sent.astype(bf16).reshape(points, 16, PLANE)
    funcs = lax.all_to_all(sent, "kq", 0, 0, tiled=True)

    ints = jnp.concatenate([here.astype(jnp.int32)[None], second])
    table = jnp.asarray(plane_table(), dtype=bf16)
    terms = pair_terms(ints, funcs, screening[0], table, amps)
    parts = lax.all_to_all(terms.reshape(points * BLOCKS, 32), ("kq", "band"), 0, 0, tiled=True)
    return jnp.sum(parts, axis=0).reshape(1, 2, 16)


def solution(mesh):
    return jax.shard_map(
        local,
        mesh=mesh,
        in_specs=(
            P("kq", None, "band", None),
            P("kq", None, None, None),
            P("kq", None, None),
            P("kq", None),
        ),
        out_specs=P("kq", None, "band"),
        check_vma=False,
    )
```

```python
import functools
import math

import jax
import jax.numpy as jnp
import numpy as np
from jax import lax
from jax.experimental import pallas as pl
from jax.experimental.pallas import tpu as pltpu
from jax.sharding import PartitionSpec as P

SIDE = 16
BOX = 8
PLANE = SIDE * SIDE
HALF = BOX * BOX
NG = BOX * HALF
BLOCKS = 4
NT = (((1,), (1,)), ((), ()))


def plane_table():
    y, z = np.divmod(np.arange(PLANE), SIDE)
    gy, gz = np.divmod(np.arange(HALF), BOX)
    m = (y[:, None] * (gy - 4)[None] + z[:, None] * (gz - 4)[None]) % SIDE
    c, s = np.cos(2 * np.pi * m / SIDE), np.sin(2 * np.pi * m / SIDE)
    top = np.concatenate([c, -s, -s, -c], axis=1)
    low = np.concatenate([s, c, c, -s], axis=1)
    return np.concatenate([top, low], axis=0)


def weighted(terms):
    total = None
    for factor, value in terms:
        if abs(factor) < 1e-9:
            continue
        if abs(abs(factor) - 1.0) < 1e-9:
            piece = value if factor > 0 else -value
        else:
            piece = value * factor
        total = piece if total is None else total + piece
    return total


def iota(shape, axis):
    return lax.broadcasted_iota(jnp.int32, shape, axis)


def second_of(seconds_ref, block, parity):
    return seconds_ref[2 * block + parity, 1]


def send_body(pairs_ref, held_ref, sent_ref):
    points = held_ref.shape[0]
    moves = [[second_of(pairs_ref, block, parity) for block in range(BLOCKS)] for parity in range(2)]
    right = [[held_ref[moves[p][b], 0:2] for b in range(BLOCKS)] for p in range(2)]

    def chip(i, carry):
        for parity in range(2):
            for block in range(BLOCKS):
                owner = 2 * i + parity
                target = owner * BLOCKS + block
                other = 2 * i + (1 - parity)
                move = moves[parity][block]
                sent_ref[target, 0] = held_ref[(owner + move) & (points - 1), 0:2]
                sent_ref[target, 1] = held_ref[(other + move) & (points - 1), 0:2]
                sent_ref[target, 2] = right[parity][block]
        return carry

    lax.fori_loop(0, points // 2, chip, 0)


def send_pieces(pairs, held, interpret=False):
    points = held.shape[0]
    vmem = pl.BlockSpec(memory_space=pltpu.VMEM)
    return pl.pallas_call(
        send_body,
        out_shape=jax.ShapeDtypeStruct((points * BLOCKS, 3, 2, 128), jnp.bfloat16),
        in_specs=[pl.BlockSpec(memory_space=pltpu.SMEM), vmem],
        out_specs=vmem,
        name="send_pieces",
        interpret=interpret,
    )(pairs, held)


def pair_body(
    place_ref,
    pairs_ref,
    funcs_ref,
    own_ref,
    other_ref,
    table_ref,
    held_ref,
    out_ref,
    dens,
    sums,
    wave_re,
    wave_im,
):
    f32, bf16 = jnp.float32, jnp.bfloat16
    points = held_ref.shape[0]

    def densities(x, carry):
        for half in range(2):
            lanes = slice(half * 128, half * 128 + 128)
            lanes_im = slice(PLANE + half * 128, PLANE + half * 128 + 128)
            for kind in range(2):

                def bands(ri, slot):
                    piece = (ri * 32 + 2 * x + half) * 2 + kind
                    return funcs_ref[pl.ds(piece * BLOCKS, BLOCKS), slot].astype(f32).reshape(8, 128)

                right_re, right_im = bands(0, 2)[None], bands(1, 2)[None]
                for pair in range(2):
                    left_re, left_im = bands(0, pair)[:, None, :], bands(1, pair)[:, None, :]
                    dens_re = (left_re * right_re + left_im * right_im).reshape(64, 128)
                    dens_im = (left_re * right_im - left_im * right_re).reshape(64, 128)
                    row = (kind * 2 + pair) * 64
                    dens[x, row : row + 64, lanes] = dens_re.astype(bf16)
                    dens[x, row : row + 64, lanes_im] = dens_im.astype(bf16)
        return carry

    lax.fori_loop(0, SIDE, densities, 0)

    def plane_sums(x, carry):
        sums[x] = jnp.dot(dens[x], table_ref[...], preferred_element_type=f32)
        return carry

    lax.fori_loop(0, SIDE, plane_sums, 0)

    scale = 1.0 / math.sqrt(SIDE**3)
    low_lanes = iota((16, 128), 1) < HALF

    def along_x(chunk, carry):
        rows = pl.ds(pl.multiple_of(chunk * 16, 16), 16)
        out = {}
        for parity in range(2):
            sign = 1.0 if parity == 0 else -1.0
            straight, turned = [], []
            for x in range(8):
                straight.append(sums[x, rows, 0:128] + sign * sums[x + 8, rows, 0:128])
                turned.append(sums[x, rows, 128:256] + sign * sums[x + 8, rows, 128:256])
            for g in (0, 2, 4) if parity == 0 else (1, 3):
                angle = [2 * math.pi * x * g / SIDE for x in range(8)]
                even = weighted([(math.cos(a), v) for a, v in zip(angle, straight)])
                odd = weighted([(math.sin(a), v) for a, v in zip(angle, turned)])
                if odd is None:
                    out[-g] = even
                else:
                    out[g], out[-g] = even + odd, even - odd
        for pair in range(4):
            first, second = out[2 * pair - 4] * scale, out[2 * pair - 3] * scale
            re = jnp.where(low_lanes, first, pltpu.roll(second, 64, 1))
            im = jnp.where(low_lanes, pltpu.roll(first, 64, 1), second)
            wave_re[rows, pair * 128 : pair * 128 + 128] = re.astype(bf16)
            wave_im[rows, pair * 128 : pair * 128 + 128] = im.astype(bf16)
        return carry

    lax.fori_loop(0, 16, along_x, 0)

    def nt(a, b):
        return lax.dot_general(a, b, NT, preferred_element_type=f32)

    here, block = place_ref[0], place_ref[1]
    move = second_of(pairs_ref, block, here & 1)
    first_point = [(here + move) & (points - 1), ((here ^ 1) + move) & (points - 1)]

    row, lane = iota((64, 128), 0), iota((64, 128), 1)
    row_hi, row_lo = row >> 3, row & 7
    q, l = iota((128, 64), 0), iota((128, 64), 1)
    pick_hi = jnp.where((q < 64) & ((q >> 3) == (l >> 3)), 1.0, 0.0).astype(bf16)
    pick_lo = jnp.where((q < 64) & ((q >> 3) == (l & 7)), 1.0, 0.0).astype(bf16)

    def spread(point, row_band, pick):
        parts = []
        for ri in range(2):
            values = held_ref[point, 2 + ri : 3 + ri].astype(f32)
            kept = jnp.where((lane & 7) == row_band, jnp.broadcast_to(values, (64, 128)), 0.0)
            parts.append(jnp.dot(kept.astype(bf16), pick, preferred_element_type=f32))
        return parts

    out_band = 2 * (lane >> 5) + ((lane >> 3) & 1)
    out_part = (lane >> 4) & 1
    out_other = lane & 7
    gather_hi = jnp.where(row_hi == out_band, 1.0, 0.0)
    gather_lo = jnp.where(row_lo == out_band, 1.0, 0.0)

    def collect(re, im, gather, row_band):
        dot = functools.partial(
            jnp.dot, precision=lax.Precision.HIGHEST, preferred_element_type=f32
        )
        both = dot(re, jnp.where(out_part == 0, gather, 0.0)) + dot(
            im, jnp.where(out_part == 1, gather, 0.0)
        )
        return jnp.sum(jnp.where(row_band == out_other, both, 0.0), axis=0, keepdims=True)

    far_re, far_im = spread(move, row_lo, pick_lo)
    r = iota((points, 128), 0)
    k = ((r & 7) << 4) | (r >> 3)
    total = jnp.zeros((points, 128), f32)
    back_re = back_im = 0.0
    for pair, weights in enumerate((own_ref, other_ref)):
        val, cond = slice(64 * pair, 64 * pair + 64), slice(128 + 64 * pair, 192 + 64 * pair)
        stacked = jnp.concatenate([wave_re[val], wave_im[val]], axis=0)
        with_re, with_im = nt(stacked, weights[0]), nt(stacked, weights[1])
        scr_re = (with_re[:64] - with_im[64:]).astype(bf16)
        scr_im = (with_re[64:] + with_im[:64]).astype(bf16)
        cond_re, cond_im = wave_re[cond], wave_im[cond]
        kern_re = (nt(cond_re, scr_re) + nt(cond_im, scr_im)) * (1.0 / NG)
        kern_im = (nt(cond_re, scr_im) - nt(cond_im, scr_re)) * (1.0 / NG)
        near_re, near_im = spread(first_point[pair], row_hi, pick_hi)
        direct = collect(
            kern_re * far_re - kern_im * far_im,
            kern_re * far_im + kern_im * far_re,
            gather_hi,
            row_hi,
        )
        back_re += kern_re * near_re + kern_im * near_im
        back_im += kern_re * near_im - kern_im * near_re
        total += jnp.where(k == first_point[pair], jnp.broadcast_to(direct, (points, 128)), 0.0)
    back = collect(back_re, back_im, gather_lo, row_lo)
    total += jnp.where(k == move, jnp.broadcast_to(back, (points, 128)), 0.0)
    out_ref[...] = total


def pair_terms(place, pairs, funcs, own, other, table, held, interpret=False):
    points = held.shape[0]
    vmem, smem = pl.BlockSpec(memory_space=pltpu.VMEM), pl.BlockSpec(memory_space=pltpu.SMEM)
    return pl.pallas_call(
        pair_body,
        out_shape=jax.ShapeDtypeStruct((points, 128), jnp.float32),
        in_specs=[smem, smem] + [vmem] * 5,
        out_specs=vmem,
        scratch_shapes=[
            pltpu.VMEM((SIDE, 256, 2 * PLANE), jnp.bfloat16),
            pltpu.VMEM((SIDE, 256, 4 * HALF), jnp.float32),
            pltpu.VMEM((256, NG), jnp.bfloat16),
            pltpu.VMEM((256, NG), jnp.bfloat16),
        ],
        compiler_params=pltpu.CompilerParams(vmem_limit_bytes=32 << 20),
        name="pair_terms",
        interpret=interpret,
    )(place, pairs, funcs, own, other, table, held)


def local(band_functions, screening, exciton, pair_list):
    bf16 = jnp.bfloat16
    points = lax.axis_size("kq")
    here, block = lax.axis_index("kq"), lax.axis_index("band")
    place = jnp.stack([here, block]).astype(jnp.int32)
    other = lax.ppermute(screening, "kq", [(i, i ^ 1) for i in range(points)])

    pieces = band_functions.reshape(2, 2, 2, 32, 128).transpose(0, 3, 1, 2, 4).reshape(points, 2, 128)
    amp_rows = jnp.pad(exciton, ((0, 0), (0, 0), (0, 64)))
    amp_rows = jnp.broadcast_to(amp_rows, (points, 2, 128))
    held = lax.all_to_all(jnp.concatenate([pieces, amp_rows], axis=1), "kq", 0, 0, tiled=True)

    funcs = lax.all_to_all(send_pieces(pair_list, held), ("kq", "band"), 0, 0, tiled=True)

    table = jnp.asarray(plane_table(), dtype=bf16)
    terms = pair_terms(place, pair_list, funcs, screening[0], other[0], table, held)

    rows = [[16 * y + z for z in range(16)] for y in range(8)]
    columns = [[(16 * y + z) * BLOCKS + b for y in range(8) for b in range(BLOCKS)] for z in range(16)]
    parts = lax.all_to_all(
        terms.reshape(16, 8, 128), "kq", 0, 0, tiled=True, axis_index_groups=rows
    )
    parts = jnp.sum(parts, axis=0).reshape(32, 1, 32)
    parts = lax.all_to_all(
        parts, ("kq", "band"), 0, 0, tiled=True, axis_index_groups=columns
    )
    return jnp.sum(parts, axis=(0, 1)).reshape(1, 2, 16)


def solution(mesh):
    return jax.shard_map(
        local,
        mesh=mesh,
        in_specs=(
            P("kq", None, "band", None),
            P("kq", None, None, None),
            P("kq", None, None),
            P("kq", None),
        ),
        out_specs=P("kq", None, "band"),
        check_vma=False,
    )
```

```python
import functools
import math

import jax
import jax.numpy as jnp
import numpy as np
from jax import lax
from jax.experimental import pallas as pl
from jax.experimental.pallas import tpu as pltpu
from jax.sharding import PartitionSpec as P

SIDE = 16
BOX = 8
PLANE = SIDE * SIDE
HALF = BOX * BOX
NG = BOX * HALF
BLOCKS = 4
NT = (((1,), (1,)), ((), ()))


def plane_table():
    y, z = np.divmod(np.arange(PLANE), SIDE)
    gy, gz = np.divmod(np.arange(HALF), BOX)
    m = (y[:, None] * (gy - 4)[None] + z[:, None] * (gz - 4)[None]) % SIDE
    c, s = np.cos(2 * np.pi * m / SIDE), np.sin(2 * np.pi * m / SIDE)
    top = np.concatenate([c, -s, -s, -c], axis=1)
    low = np.concatenate([s, c, c, -s], axis=1)
    return np.concatenate([top, low], axis=0)


def weighted(terms):
    total = None
    for factor, value in terms:
        if abs(factor) < 1e-9:
            continue
        if abs(abs(factor) - 1.0) < 1e-9:
            piece = value if factor > 0 else -value
        else:
            piece = value * factor
        total = piece if total is None else total + piece
    return total


def iota(shape, axis):
    return lax.broadcasted_iota(jnp.int32, shape, axis)


def second_of(seconds_ref, block, parity):
    return seconds_ref[2 * block + parity, 1]


def pack_body(pieces_ref, exciton_ref, packed_ref):
    points = pieces_ref.shape[0]
    amps = jnp.concatenate([exciton_ref[0], jnp.zeros((2, 64), jnp.bfloat16)], axis=1)
    packed_ref[:, 0:2] = pieces_ref[...]
    packed_ref[:, 2:4] = jnp.broadcast_to(amps[None], (points, 2, 128))


def pack_pieces(pieces, exciton, interpret=False):
    points = pieces.shape[0]
    vmem = pl.BlockSpec(memory_space=pltpu.VMEM)
    return pl.pallas_call(
        pack_body,
        out_shape=jax.ShapeDtypeStruct((points, 4, 128), jnp.bfloat16),
        in_specs=[vmem, vmem],
        out_specs=vmem,
        compiler_params=pltpu.CompilerParams(vmem_limit_bytes=4 << 20),
        name="pack_pieces",
        interpret=interpret,
    )(pieces, exciton)


def send_body(pairs_ref, held_ref, sent_ref, twice):
    points = held_ref.shape[0]
    twice[0:points] = held_ref[...]
    twice[points : 2 * points] = held_ref[...]
    moves = [[second_of(pairs_ref, block, parity) for block in range(BLOCKS)] for parity in range(2)]
    right = [[held_ref[moves[p][b], 0:2] for b in range(BLOCKS)] for p in range(2)]

    def chip(i, carry):
        for parity in range(2):
            for block in range(BLOCKS):
                target = (2 * i + parity) * BLOCKS + block
                run = 2 * i + moves[parity][block]
                sent_ref[target, 0] = twice[run + parity, 0:2]
                sent_ref[target, 1] = twice[run + (1 - parity), 0:2]
                sent_ref[target, 2] = right[parity][block]
        return carry

    lax.fori_loop(0, points // 2, chip, 0, unroll=2)


def send_pieces(pairs, held, interpret=False):
    points = held.shape[0]
    vmem = pl.BlockSpec(memory_space=pltpu.VMEM)
    return pl.pallas_call(
        send_body,
        out_shape=jax.ShapeDtypeStruct((points * BLOCKS, 3, 2, 128), jnp.bfloat16),
        in_specs=[pl.BlockSpec(memory_space=pltpu.SMEM), vmem],
        out_specs=vmem,
        scratch_shapes=[pltpu.VMEM((2 * points, 4, 128), jnp.bfloat16)],
        compiler_params=pltpu.CompilerParams(vmem_limit_bytes=4 << 20),
        name="send_pieces",
        interpret=interpret,
    )(pairs, held)


def pair_body(
    place_ref,
    pairs_ref,
    funcs_ref,
    own_ref,
    other_ref,
    table_ref,
    held_ref,
    out_ref,
    dens_even,
    dens_odd,
    sums,
    wave_re,
    wave_im,
):
    f32, bf16 = jnp.float32, jnp.bfloat16
    points = held_ref.shape[0]

    def densities(x, dens):
        for half in range(2):
            lanes = slice(half * 128, half * 128 + 128)
            lanes_im = slice(PLANE + half * 128, PLANE + half * 128 + 128)
            for kind in range(2):

                def bands(ri, slot):
                    piece = (ri * 32 + 2 * x + half) * 2 + kind
                    return funcs_ref[pl.ds(piece * BLOCKS, BLOCKS), slot].astype(f32).reshape(8, 128)

                right_re, right_im = bands(0, 2)[None], bands(1, 2)[None]
                for pair in range(2):
                    left_re, left_im = bands(0, pair)[:, None, :], bands(1, pair)[:, None, :]
                    dens_re = (left_re * right_re + left_im * right_im).reshape(64, 128)
                    dens_im = (left_re * right_im - left_im * right_re).reshape(64, 128)
                    row = (kind * 2 + pair) * 64
                    dens[row : row + 64, lanes] = dens_re.astype(bf16)
                    dens[row : row + 64, lanes_im] = dens_im.astype(bf16)

    densities(0, dens_even)

    def planes(i, carry):
        x = 2 * i
        sums[x] = jnp.dot(dens_even[...], table_ref[...], preferred_element_type=f32)
        densities(x + 1, dens_odd)
        sums[x + 1] = jnp.dot(dens_odd[...], table_ref[...], preferred_element_type=f32)
        densities(jnp.minimum(x + 2, SIDE - 1), dens_even)
        return carry

    lax.fori_loop(0, SIDE // 2, planes, 0)

    scale = 1.0 / math.sqrt(SIDE**3)
    low_lanes = iota((16, 128), 1) < HALF

    def along_x(chunk, carry):
        rows = pl.ds(pl.multiple_of(chunk * 16, 16), 16)
        out = {}
        for parity in range(2):
            sign = 1.0 if parity == 0 else -1.0
            straight, turned = [], []
            for x in range(8):
                straight.append(sums[x, rows, 0:128] + sign * sums[x + 8, rows, 0:128])
                turned.append(sums[x, rows, 128:256] + sign * sums[x + 8, rows, 128:256])
            for g in (0, 2, 4) if parity == 0 else (1, 3):
                angle = [2 * math.pi * x * g / SIDE for x in range(8)]
                even = weighted([(math.cos(a), v) for a, v in zip(angle, straight)])
                odd = weighted([(math.sin(a), v) for a, v in zip(angle, turned)])
                if odd is None:
                    out[-g] = even
                else:
                    out[g], out[-g] = even + odd, even - odd
        for pair in range(4):
            first, second = out[2 * pair - 4] * scale, out[2 * pair - 3] * scale
            re = jnp.where(low_lanes, first, pltpu.roll(second, 64, 1))
            im = jnp.where(low_lanes, pltpu.roll(first, 64, 1), second)
            wave_re[rows, pair * 128 : pair * 128 + 128] = re.astype(bf16)
            wave_im[rows, pair * 128 : pair * 128 + 128] = im.astype(bf16)
        return carry

    lax.fori_loop(0, 16, along_x, 0)

    def nt(a, b):
        return lax.dot_general(a, b, NT, preferred_element_type=f32)

    here, block = place_ref[0], place_ref[1]
    move = second_of(pairs_ref, block, here & 1)
    first_point = [(here + move) & (points - 1), ((here ^ 1) + move) & (points - 1)]

    row, lane = iota((64, 128), 0), iota((64, 128), 1)
    row_hi, row_lo = row >> 3, row & 7
    q, l = iota((128, 64), 0), iota((128, 64), 1)
    pick_hi = jnp.where((q < 64) & ((q >> 3) == (l >> 3)), 1.0, 0.0).astype(bf16)
    pick_lo = jnp.where((q < 64) & ((q >> 3) == (l & 7)), 1.0, 0.0).astype(bf16)

    def spread(point, row_band, pick):
        parts = []
        for ri in range(2):
            values = held_ref[point, 2 + ri : 3 + ri].astype(f32)
            kept = jnp.where((lane & 7) == row_band, jnp.broadcast_to(values, (64, 128)), 0.0)
            parts.append(jnp.dot(kept.astype(bf16), pick, preferred_element_type=f32))
        return parts

    out_band = 2 * (lane >> 5) + ((lane >> 3) & 1)
    out_part = (lane >> 4) & 1
    out_other = lane & 7
    gather_hi = jnp.where(row_hi == out_band, 1.0, 0.0)
    gather_lo = jnp.where(row_lo == out_band, 1.0, 0.0)

    def collect(re, im, gather, row_band):
        dot = functools.partial(
            jnp.dot, precision=lax.Precision.HIGHEST, preferred_element_type=f32
        )
        both = dot(re, jnp.where(out_part == 0, gather, 0.0)) + dot(
            im, jnp.where(out_part == 1, gather, 0.0)
        )
        return jnp.sum(jnp.where(row_band == out_other, both, 0.0), axis=0, keepdims=True)

    far_re, far_im = spread(move, row_lo, pick_lo)
    r = iota((points, 128), 0)
    k = ((r & 7) << 4) | (r >> 3)
    total = jnp.zeros((points, 128), f32)
    back_re = back_im = 0.0
    for pair, weights in enumerate((own_ref, other_ref)):
        val, cond = slice(64 * pair, 64 * pair + 64), slice(128 + 64 * pair, 192 + 64 * pair)
        stacked = jnp.concatenate([wave_re[val], wave_im[val]], axis=0)
        with_re, with_im = nt(stacked, weights[0]), nt(stacked, weights[1])
        scr_re = (with_re[:64] - with_im[64:]).astype(bf16)
        scr_im = (with_re[64:] + with_im[:64]).astype(bf16)
        cond_re, cond_im = wave_re[cond], wave_im[cond]
        kern_re = (nt(cond_re, scr_re) + nt(cond_im, scr_im)) * (1.0 / NG)
        kern_im = (nt(cond_re, scr_im) - nt(cond_im, scr_re)) * (1.0 / NG)
        near_re, near_im = spread(first_point[pair], row_hi, pick_hi)
        direct = collect(
            kern_re * far_re - kern_im * far_im,
            kern_re * far_im + kern_im * far_re,
            gather_hi,
            row_hi,
        )
        back_re += kern_re * near_re + kern_im * near_im
        back_im += kern_re * near_im - kern_im * near_re
        total += jnp.where(k == first_point[pair], jnp.broadcast_to(direct, (points, 128)), 0.0)
    back = collect(back_re, back_im, gather_lo, row_lo)
    total += jnp.where(k == move, jnp.broadcast_to(back, (points, 128)), 0.0)
    out_ref[...] = total


def pair_terms(place, pairs, funcs, own, other, table, held, interpret=False):
    points = held.shape[0]
    vmem, smem = pl.BlockSpec(memory_space=pltpu.VMEM), pl.BlockSpec(memory_space=pltpu.SMEM)
    return pl.pallas_call(
        pair_body,
        out_shape=jax.ShapeDtypeStruct((points, 128), jnp.float32),
        in_specs=[smem, smem] + [vmem] * 5,
        out_specs=vmem,
        scratch_shapes=[
            pltpu.VMEM((256, 2 * PLANE), jnp.bfloat16),
            pltpu.VMEM((256, 2 * PLANE), jnp.bfloat16),
            pltpu.VMEM((SIDE, 256, 4 * HALF), jnp.float32),
            pltpu.VMEM((256, NG), jnp.bfloat16),
            pltpu.VMEM((256, NG), jnp.bfloat16),
        ],
        compiler_params=pltpu.CompilerParams(vmem_limit_bytes=32 << 20),
        name="pair_terms",
        interpret=interpret,
    )(place, pairs, funcs, own, other, table, held)


def local(band_functions, screening, exciton, pair_list):
    bf16 = jnp.bfloat16
    points = lax.axis_size("kq")
    here, block = lax.axis_index("kq"), lax.axis_index("band")
    place = jnp.stack([here, block]).astype(jnp.int32)
    other = lax.ppermute(screening, "kq", [(i, i ^ 1) for i in range(points)])

    pieces = band_functions.reshape(2, 2, 2, 32, 128).transpose(0, 3, 1, 2, 4).reshape(points, 2, 128)
    held = lax.all_to_all(pack_pieces(pieces, exciton), "kq", 0, 0, tiled=True)

    funcs = lax.all_to_all(send_pieces(pair_list, held), ("kq", "band"), 0, 0, tiled=True)

    table = jnp.asarray(plane_table(), dtype=bf16)
    terms = pair_terms(place, pair_list, funcs, screening[0], other[0], table, held)

    rows = [[16 * y + z for z in range(16)] for y in range(8)]
    columns = [[(16 * y + z) * BLOCKS + b for y in range(8) for b in range(BLOCKS)] for z in range(16)]
    parts = lax.all_to_all(
        terms.reshape(16, 8, 128), "kq", 0, 0, tiled=True, axis_index_groups=rows
    )
    parts = jnp.sum(parts, axis=0).reshape(32, 1, 32)
    parts = lax.all_to_all(
        parts, ("kq", "band"), 0, 0, tiled=True, axis_index_groups=columns
    )
    return jnp.sum(parts, axis=(0, 1)).reshape(1, 2, 16)


def solution(mesh):
    return jax.shard_map(
        local,
        mesh=mesh,
        in_specs=(
            P("kq", None, "band", None),
            P("kq", None, None, None),
            P("kq", None, None),
            P("kq", None),
        ),
        out_specs=P("kq", None, "band"),
        check_vma=False,
    )
```

```python
import functools
import math

import jax
import jax.numpy as jnp
import numpy as np
from jax import lax
from jax.experimental import pallas as pl
from jax.experimental.pallas import tpu as pltpu
from jax.sharding import PartitionSpec as P

SIDE = 16
BOX = 8
PLANE = SIDE * SIDE
HALF = BOX * BOX
NG = BOX * HALF
BLOCKS = 4
NT = (((1,), (1,)), ((), ()))


def plane_table():
    y, z = np.divmod(np.arange(PLANE), SIDE)
    gy, gz = np.divmod(np.arange(HALF), BOX)
    m = (y[:, None] * (gy - 4)[None] + z[:, None] * (gz - 4)[None]) % SIDE
    c, s = np.cos(2 * np.pi * m / SIDE), np.sin(2 * np.pi * m / SIDE)
    top = np.concatenate([c, -s, -s, -c], axis=1)
    low = np.concatenate([s, c, c, -s], axis=1)
    return np.concatenate([top, low], axis=0)


def weighted(terms):
    total = None
    for factor, value in terms:
        if abs(factor) < 1e-9:
            continue
        if abs(abs(factor) - 1.0) < 1e-9:
            piece = value if factor > 0 else -value
        else:
            piece = value * factor
        total = piece if total is None else total + piece
    return total


def iota(shape, axis):
    return lax.broadcasted_iota(jnp.int32, shape, axis)


def second_of(seconds_ref, block, parity):
    return seconds_ref[2 * block + parity, 1]


def pack_body(pieces_ref, exciton_ref, packed_ref):
    points = pieces_ref.shape[0]
    amps = jnp.concatenate([exciton_ref[0], jnp.zeros((2, 64), jnp.bfloat16)], axis=1)
    packed_ref[:, 0:2] = pieces_ref[...]
    packed_ref[:, 2:4] = jnp.broadcast_to(amps[None], (points, 2, 128))


def pack_pieces(pieces, exciton, interpret=False):
    points = pieces.shape[0]
    vmem = pl.BlockSpec(memory_space=pltpu.VMEM)
    return pl.pallas_call(
        pack_body,
        out_shape=jax.ShapeDtypeStruct((points, 4, 128), jnp.bfloat16),
        in_specs=[vmem, vmem],
        out_specs=vmem,
        name="pack_pieces",
        interpret=interpret,
    )(pieces, exciton)


def send_body(pairs_ref, held_ref, sent_ref, twice):
    points = held_ref.shape[0]
    twice[0:points] = held_ref[...]
    twice[points : 2 * points] = held_ref[...]
    moves = [[second_of(pairs_ref, block, parity) for block in range(BLOCKS)] for parity in range(2)]
    right = [[held_ref[moves[p][b], 0:2] for b in range(BLOCKS)] for p in range(2)]

    def chip(i, carry):
        for parity in range(2):
            for block in range(BLOCKS):
                target = (2 * i + parity) * BLOCKS + block
                run = 2 * i + moves[parity][block]
                sent_ref[target, 0] = twice[run + parity, 0:2]
                sent_ref[target, 1] = twice[run + (1 - parity), 0:2]
                sent_ref[target, 2] = right[parity][block]
        return carry

    lax.fori_loop(0, points // 2, chip, 0, unroll=2)


def send_pieces(pairs, held, interpret=False):
    points = held.shape[0]
    vmem = pl.BlockSpec(memory_space=pltpu.VMEM)
    return pl.pallas_call(
        send_body,
        out_shape=jax.ShapeDtypeStruct((points * BLOCKS, 3, 2, 128), jnp.bfloat16),
        in_specs=[pl.BlockSpec(memory_space=pltpu.SMEM), vmem],
        out_specs=vmem,
        scratch_shapes=[pltpu.VMEM((2 * points, 4, 128), jnp.bfloat16)],
        compiler_params=pltpu.CompilerParams(vmem_limit_bytes=4 << 20),
        name="send_pieces",
        interpret=interpret,
    )(pairs, held)


def pair_body(
    place_ref,
    pairs_ref,
    funcs_ref,
    own_ref,
    other_ref,
    table_ref,
    held_ref,
    out_ref,
    dens_even,
    dens_odd,
    left_even,
    left_odd,
    sums,
    wave_re,
    wave_im,
):
    f32, bf16 = jnp.float32, jnp.bfloat16
    points = held_ref.shape[0]

    def densities(x, dens, left):
        for kind in range(2):

            def bands(ri, slot):
                parts = []
                for half in range(2):
                    piece = (ri * 32 + 2 * x + half) * 2 + kind
                    part = funcs_ref[pl.ds(piece * BLOCKS, BLOCKS), slot]
                    parts.append(part.astype(f32).reshape(8, 128))
                return jnp.concatenate(parts, axis=1)

            right_re, right_im = bands(0, 2), bands(1, 2)
            for pair in range(2):
                place = (kind * 2 + pair) * 16
                left[place : place + 8] = bands(0, pair)
                left[place + 8 : place + 16] = bands(1, pair)
                for v in range(8):
                    left_re = left[pl.ds(place + v, 8, stride=0)]
                    left_im = left[pl.ds(place + 8 + v, 8, stride=0)]
                    row = (kind * 2 + pair) * 64 + 8 * v
                    dens_re = left_re * right_re + left_im * right_im
                    dens_im = left_re * right_im - left_im * right_re
                    dens[row : row + 8, :PLANE] = dens_re.astype(bf16)
                    dens[row : row + 8, PLANE:] = dens_im.astype(bf16)

    densities(0, dens_even, left_even)

    def planes(i, carry):
        x = 2 * i
        sums[x] = jnp.dot(dens_even[...], table_ref[...], preferred_element_type=f32)
        densities(x + 1, dens_odd, left_odd)
        sums[x + 1] = jnp.dot(dens_odd[...], table_ref[...], preferred_element_type=f32)
        densities(jnp.minimum(x + 2, SIDE - 1), dens_even, left_even)
        return carry

    lax.fori_loop(0, SIDE // 2, planes, 0)

    scale = 1.0 / math.sqrt(SIDE**3)
    low_lanes = iota((16, 128), 1) < HALF

    def along_x(chunk, carry):
        rows = pl.ds(pl.multiple_of(chunk * 16, 16), 16)
        out = {}
        for parity in range(2):
            sign = 1.0 if parity == 0 else -1.0
            straight, turned = [], []
            for x in range(8):
                straight.append(sums[x, rows, 0:128] + sign * sums[x + 8, rows, 0:128])
                turned.append(sums[x, rows, 128:256] + sign * sums[x + 8, rows, 128:256])
            for g in (0, 2, 4) if parity == 0 else (1, 3):
                angle = [2 * math.pi * x * g / SIDE for x in range(8)]
                even = weighted([(math.cos(a), v) for a, v in zip(angle, straight)])
                odd = weighted([(math.sin(a), v) for a, v in zip(angle, turned)])
                if odd is None:
                    out[-g] = even
                else:
                    out[g], out[-g] = even + odd, even - odd
        for pair in range(4):
            first, second = out[2 * pair - 4] * scale, out[2 * pair - 3] * scale
            re = jnp.where(low_lanes, first, pltpu.roll(second, 64, 1))
            im = jnp.where(low_lanes, pltpu.roll(first, 64, 1), second)
            wave_re[rows, pair * 128 : pair * 128 + 128] = re.astype(bf16)
            wave_im[rows, pair * 128 : pair * 128 + 128] = im.astype(bf16)
        return carry

    lax.fori_loop(0, 16, along_x, 0)

    def nt(a, b):
        return lax.dot_general(a, b, NT, preferred_element_type=f32)

    here, block = place_ref[0], place_ref[1]
    move = second_of(pairs_ref, block, here & 1)
    first_point = [(here + move) & (points - 1), ((here ^ 1) + move) & (points - 1)]

    row, lane = iota((64, 128), 0), iota((64, 128), 1)
    row_hi, row_lo = row >> 3, row & 7
    q, l = iota((128, 128), 0), iota((128, 128), 1)
    pick_hi = jnp.where((q >> 3) == ((l >> 3) & 7), 1.0, 0.0).astype(bf16)
    pick_lo = jnp.where((q >> 3) == (l & 7), 1.0, 0.0).astype(bf16)

    def rows_of(point, row_band):
        kept = []
        for ri in range(2):
            values = jnp.broadcast_to(held_ref[point, 2 + ri : 3 + ri].astype(f32), (64, 128))
            kept.append(jnp.where((lane & 7) == row_band, values, 0.0))
        return kept

    def spread(kept, pick):
        kept = jnp.concatenate(kept, axis=0).astype(bf16)
        return jnp.dot(kept, pick, preferred_element_type=f32)

    far = spread(rows_of(move, row_lo), pick_lo)
    near = spread(rows_of(first_point[0], row_hi) + rows_of(first_point[1], row_hi), pick_hi)
    minus_low = jnp.where(lane < 64, -1.0, 1.0)
    far_re, far_im = far[:64], far[64:] * minus_low

    out_band = 2 * (l >> 5) + ((l >> 3) & 1)
    out_part = (l >> 4) & 1
    part = (q >> 6) == out_part
    gather_hi = jnp.where(part & (((q >> 3) & 7) == out_band), 1.0, 0.0).astype(bf16)
    gather_lo = jnp.where(part & ((q & 7) == out_band), 1.0, 0.0).astype(bf16)

    def collect(values, gather, row_band):
        high = values.astype(bf16)
        rest = values - high.astype(f32)
        middle = rest.astype(bf16)
        low = (rest - middle.astype(f32)).astype(bf16)
        both = sum(jnp.dot(p, gather, preferred_element_type=f32) for p in (high, middle, low))
        return jnp.sum(jnp.where(row_band == (lane & 7), both, 0.0), axis=0, keepdims=True)

    r = iota((points, 128), 0)
    k = ((r & 7) << 4) | (r >> 3)
    total = jnp.zeros((points, 128), f32)
    back = 0.0
    for pair, weights in enumerate((own_ref, other_ref)):
        val, cond = slice(64 * pair, 64 * pair + 64), slice(128 + 64 * pair, 192 + 64 * pair)
        stacked = jnp.concatenate([wave_re[val], wave_im[val]], axis=0)
        with_re, with_im = nt(stacked, weights[0]), nt(stacked, weights[1])
        scr_re, scr_im = with_re[:64] - with_im[64:], with_re[64:] + with_im[:64]
        straight = jnp.concatenate([scr_re, scr_im], axis=0).astype(bf16)
        turned = jnp.concatenate([scr_im, -scr_re], axis=0).astype(bf16)
        kern = (nt(wave_re[cond], straight) + nt(wave_im[cond], turned)) * (1.0 / NG)
        swapped = pltpu.roll(kern, 64, 1)
        near_re, near_im = near[128 * pair : 128 * pair + 64], near[128 * pair + 64 : 128 * pair + 128]
        direct = collect(kern * far_re + swapped * far_im, gather_hi, row_hi)
        back += swapped * near_im - kern * (near_re * minus_low)
        total += jnp.where(k == first_point[pair], jnp.broadcast_to(direct, (points, 128)), 0.0)
    back = collect(back, gather_lo, row_lo)
    total += jnp.where(k == move, jnp.broadcast_to(back, (points, 128)), 0.0)
    out_ref[...] = total


def pair_terms(place, pairs, funcs, own, other, table, held, interpret=False):
    points = held.shape[0]
    vmem, smem = pl.BlockSpec(memory_space=pltpu.VMEM), pl.BlockSpec(memory_space=pltpu.SMEM)
    return pl.pallas_call(
        pair_body,
        out_shape=jax.ShapeDtypeStruct((points, 128), jnp.float32),
        in_specs=[smem, smem] + [vmem] * 5,
        out_specs=vmem,
        scratch_shapes=[
            pltpu.VMEM((256, 2 * PLANE), jnp.bfloat16),
            pltpu.VMEM((256, 2 * PLANE), jnp.bfloat16),
            pltpu.VMEM((72, PLANE), jnp.float32),
            pltpu.VMEM((72, PLANE), jnp.float32),
            pltpu.VMEM((SIDE, 256, 4 * HALF), jnp.float32),
            pltpu.VMEM((256, NG), jnp.bfloat16),
            pltpu.VMEM((256, NG), jnp.bfloat16),
        ],
        compiler_params=pltpu.CompilerParams(vmem_limit_bytes=32 << 20),
        name="pair_terms",
        interpret=interpret,
    )(place, pairs, funcs, own, other, table, held)


def local(band_functions, screening, exciton, pair_list):
    bf16 = jnp.bfloat16
    points = lax.axis_size("kq")
    here, block = lax.axis_index("kq"), lax.axis_index("band")
    place = jnp.stack([here, block]).astype(jnp.int32)
    other = lax.ppermute(screening, "kq", [(i, i ^ 1) for i in range(points)])

    pieces = band_functions.reshape(2, 2, 2, 32, 128).transpose(0, 3, 1, 2, 4).reshape(points, 2, 128)
    held = lax.all_to_all(pack_pieces(pieces, exciton), "kq", 0, 0, tiled=True)

    funcs = lax.all_to_all(send_pieces(pair_list, held), ("kq", "band"), 0, 0, tiled=True)

    table = jnp.asarray(plane_table(), dtype=bf16)
    terms = pair_terms(place, pair_list, funcs, screening[0], other[0], table, held)

    rows = [[16 * y + z for z in range(16)] for y in range(8)]
    columns = [[(16 * y + z) * BLOCKS + b for y in range(8) for b in range(BLOCKS)] for z in range(16)]
    parts = lax.all_to_all(
        terms.reshape(16, 8, 128), "kq", 0, 0, tiled=True, axis_index_groups=rows
    )
    parts = jnp.sum(parts, axis=0).reshape(32, 1, 32)
    parts = lax.all_to_all(
        parts, ("kq", "band"), 0, 0, tiled=True, axis_index_groups=columns
    )
    return jnp.sum(parts, axis=(0, 1)).reshape(1, 2, 16)


def solution(mesh):
    return jax.shard_map(
        local,
        mesh=mesh,
        in_specs=(
            P("kq", None, "band", None),
            P("kq", None, None, None),
            P("kq", None, None),
            P("kq", None),
        ),
        out_specs=P("kq", None, "band"),
        check_vma=False,
    )
```

```python
import functools
import math

import jax
import jax.numpy as jnp
import numpy as np
from jax import lax
from jax.experimental import pallas as pl
from jax.experimental.pallas import tpu as pltpu
from jax.sharding import PartitionSpec as P

SIDE = 16
BOX = 8
PLANE = SIDE * SIDE
HALF = BOX * BOX
NG = BOX * HALF
BLOCKS = 4
QUARTERS = 4
AT_ONCE = 2
NT = (((1,), (1,)), ((), ()))


def plane_table():
    y, z = np.divmod(np.arange(PLANE), SIDE)
    gy, gz = np.divmod(np.arange(HALF), BOX)
    m = (y[:, None] * (gy - 4)[None] + z[:, None] * (gz - 4)[None]) % SIDE
    c, s = np.cos(2 * np.pi * m / SIDE), np.sin(2 * np.pi * m / SIDE)
    top = np.concatenate([c, -s, -s, -c], axis=1)
    low = np.concatenate([s, c, c, -s], axis=1)
    return np.concatenate([top, low], axis=0)


def weighted(terms):
    total = None
    for factor, value in terms:
        if abs(factor) < 1e-9:
            continue
        if abs(abs(factor) - 1.0) < 1e-9:
            piece = value if factor > 0 else -value
        else:
            piece = value * factor
        total = piece if total is None else total + piece
    return total


def iota(shape, axis):
    return lax.broadcasted_iota(jnp.int32, shape, axis)


def second_of(seconds_ref, block, parity):
    return seconds_ref[2 * block + parity, 1]


def pack_body(pieces_ref, exciton_ref, packed_ref):
    points = pieces_ref.shape[0]
    amps = jnp.concatenate([exciton_ref[0], jnp.zeros((2, 64), jnp.bfloat16)], axis=1)
    packed_ref[:, 0:2] = pieces_ref[...]
    packed_ref[:, 2:4] = jnp.broadcast_to(amps[None], (points, 2, 128))


def pack_pieces(pieces, exciton, interpret=False):
    points = pieces.shape[0]
    vmem = pl.BlockSpec(memory_space=pltpu.VMEM)
    return pl.pallas_call(
        pack_body,
        out_shape=jax.ShapeDtypeStruct((points, 4, 128), jnp.bfloat16),
        in_specs=[vmem, vmem],
        out_specs=vmem,
        name="pack_pieces",
        interpret=interpret,
    )(pieces, exciton)


def send_body(pairs_ref, held_ref, sent_ref, twice, built, done):
    points = held_ref.shape[0]
    part = built.shape[0] // QUARTERS
    twice[0:points] = held_ref[...]
    twice[points : 2 * points] = held_ref[...]
    moves = [[second_of(pairs_ref, block, parity) for block in range(BLOCKS)] for parity in range(2)]
    right = [[held_ref[moves[p][b], 0:2] for b in range(BLOCKS)] for p in range(2)]

    def chip(i, carry):
        for parity in range(2):
            for block in range(BLOCKS):
                target = (2 * i + parity) * BLOCKS + block
                run = 2 * i + moves[parity][block]
                built[target, 0] = twice[run + parity, 0:2]
                built[target, 1] = twice[run + (1 - parity), 0:2]
                built[target, 2] = right[parity][block]
        return carry

    copies = []
    chips = points // (2 * QUARTERS)
    for quarter in range(QUARTERS):
        lax.fori_loop(quarter * chips, (quarter + 1) * chips, chip, 0, unroll=2)
        rows = pl.ds(quarter * part, part)
        copies.append(pltpu.make_async_copy(built.at[rows], sent_ref.at[rows], done.at[quarter]))
        copies[-1].start()
    for copy in copies:
        copy.wait()


def send_pieces(pairs, held, interpret=False):
    points = held.shape[0]
    shape = (points * BLOCKS, 3, 2, 128)
    return pl.pallas_call(
        send_body,
        out_shape=jax.ShapeDtypeStruct(shape, jnp.bfloat16),
        in_specs=[
            pl.BlockSpec(memory_space=pltpu.SMEM),
            pl.BlockSpec(memory_space=pltpu.VMEM),
        ],
        out_specs=pl.BlockSpec(memory_space=pl.ANY),
        scratch_shapes=[
            pltpu.VMEM((2 * points, 4, 128), jnp.bfloat16),
            pltpu.VMEM(shape, jnp.bfloat16),
            pltpu.SemaphoreType.DMA((QUARTERS,)),
        ],
        compiler_params=pltpu.CompilerParams(vmem_limit_bytes=4 << 20),
        name="send_pieces",
        interpret=interpret,
    )(pairs, held)


def pair_body(
    place_ref,
    pairs_ref,
    funcs_ref,
    own_ref,
    other_ref,
    table_ref,
    held_ref,
    out_ref,
    dens_even,
    dens_odd,
    left_even,
    left_odd,
    sums,
    wave_re,
    wave_im,
):
    f32, bf16 = jnp.float32, jnp.bfloat16
    points = held_ref.shape[0]

    def densities(x, dens, left):
        for kind in range(2):

            def bands(ri, slot):
                parts = []
                for half in range(2):
                    piece = (ri * 32 + 2 * x + half) * 2 + kind
                    part = funcs_ref[pl.ds(piece * BLOCKS, BLOCKS), slot]
                    parts.append(part.astype(f32).reshape(8, 128))
                return jnp.concatenate(parts, axis=1)

            right_re, right_im = bands(0, 2), bands(1, 2)
            for pair in range(2):
                place = (kind * 2 + pair) * 16
                left[place : place + 8] = bands(0, pair)
                left[place + 8 : place + 16] = bands(1, pair)
                for v in range(8):
                    left_re = left[pl.ds(place + v, 8, stride=0)]
                    left_im = left[pl.ds(place + 8 + v, 8, stride=0)]
                    row = (kind * 2 + pair) * 64 + 8 * v
                    dens_re = left_re * right_re + left_im * right_im
                    dens_im = left_re * right_im - left_im * right_re
                    dens[row : row + 8, :PLANE] = dens_re.astype(bf16)
                    dens[row : row + 8, PLANE:] = dens_im.astype(bf16)

    def fill(x, dens, left):
        for i in range(AT_ONCE):
            densities(x + i, dens.at[pl.ds(256 * i, 256)], left)

    def sum_up(x, dens):
        both = jnp.dot(dens[...], table_ref[...], preferred_element_type=f32)
        for i in range(AT_ONCE):
            sums[x + i] = both[256 * i : 256 * i + 256]

    fill(0, dens_even, left_even)

    def planes(i, carry):
        x = 2 * AT_ONCE * i
        sum_up(x, dens_even)
        fill(x + AT_ONCE, dens_odd, left_odd)
        sum_up(x + AT_ONCE, dens_odd)
        fill(jnp.minimum(x + 2 * AT_ONCE, SIDE - AT_ONCE), dens_even, left_even)
        return carry

    lax.fori_loop(0, SIDE // (2 * AT_ONCE), planes, 0)

    scale = 1.0 / math.sqrt(SIDE**3)
    low_lanes = iota((16, 128), 1) < HALF

    def along_x(chunk, carry):
        rows = pl.ds(pl.multiple_of(chunk * 16, 16), 16)
        out = {}
        for parity in range(2):
            sign = 1.0 if parity == 0 else -1.0
            straight, turned = [], []
            for x in range(8):
                straight.append(sums[x, rows, 0:128] + sign * sums[x + 8, rows, 0:128])
                turned.append(sums[x, rows, 128:256] + sign * sums[x + 8, rows, 128:256])
            for g in (0, 2, 4) if parity == 0 else (1, 3):
                angle = [2 * math.pi * x * g / SIDE for x in range(8)]
                even = weighted([(math.cos(a), v) for a, v in zip(angle, straight)])
                odd = weighted([(math.sin(a), v) for a, v in zip(angle, turned)])
                if odd is None:
                    out[-g] = even
                else:
                    out[g], out[-g] = even + odd, even - odd
        for pair in range(4):
            first, second = out[2 * pair - 4] * scale, out[2 * pair - 3] * scale
            re = jnp.where(low_lanes, first, pltpu.roll(second, 64, 1))
            im = jnp.where(low_lanes, pltpu.roll(first, 64, 1), second)
            wave_re[rows, pair * 128 : pair * 128 + 128] = re.astype(bf16)
            wave_im[rows, pair * 128 : pair * 128 + 128] = im.astype(bf16)
        return carry

    lax.fori_loop(0, 16, along_x, 0)

    def nt(a, b):
        return lax.dot_general(a, b, NT, preferred_element_type=f32)

    here, block = place_ref[0], place_ref[1]
    move = second_of(pairs_ref, block, here & 1)
    first_point = [(here + move) & (points - 1), ((here ^ 1) + move) & (points - 1)]

    row, lane = iota((64, 128), 0), iota((64, 128), 1)
    row_hi, row_lo = row >> 3, row & 7
    q, l = iota((128, 128), 0), iota((128, 128), 1)
    pick_hi = jnp.where((q >> 3) == ((l >> 3) & 7), 1.0, 0.0).astype(bf16)
    pick_lo = jnp.where((q >> 3) == (l & 7), 1.0, 0.0).astype(bf16)

    def rows_of(point, row_band):
        kept = []
        for ri in range(2):
            values = jnp.broadcast_to(held_ref[point, 2 + ri : 3 + ri].astype(f32), (64, 128))
            kept.append(jnp.where((lane & 7) == row_band, values, 0.0))
        return kept

    def spread(kept, pick):
        kept = jnp.concatenate(kept, axis=0).astype(bf16)
        return jnp.dot(kept, pick, preferred_element_type=f32)

    far = spread(rows_of(move, row_lo), pick_lo)
    near = spread(rows_of(first_point[0], row_hi) + rows_of(first_point[1], row_hi), pick_hi)
    minus_low = jnp.where(lane < 64, -1.0, 1.0)
    far_re, far_im = far[:64], far[64:] * minus_low

    out_band = 2 * (l >> 5) + ((l >> 3) & 1)
    out_part = (l >> 4) & 1
    part = (q >> 6) == out_part
    gather_hi = jnp.where(part & (((q >> 3) & 7) == out_band), 1.0, 0.0).astype(bf16)
    gather_lo = jnp.where(part & ((q & 7) == out_band), 1.0, 0.0).astype(bf16)

    def collect(values, gather, row_band):
        high = values.astype(bf16)
        rest = values - high.astype(f32)
        middle = rest.astype(bf16)
        low = (rest - middle.astype(f32)).astype(bf16)
        both = sum(jnp.dot(p, gather, preferred_element_type=f32) for p in (high, middle, low))
        return jnp.sum(jnp.where(row_band == (lane & 7), both, 0.0), axis=0, keepdims=True)

    r = iota((points, 128), 0)
    k = ((r & 7) << 4) | (r >> 3)
    total = jnp.zeros((points, 128), f32)
    back = 0.0
    for pair, weights in enumerate((own_ref, other_ref)):
        val, cond = slice(64 * pair, 64 * pair + 64), slice(128 + 64 * pair, 192 + 64 * pair)
        stacked = jnp.concatenate([wave_re[val], wave_im[val]], axis=0)
        with_re, with_im = nt(stacked, weights[0]), nt(stacked, weights[1])
        scr_re, scr_im = with_re[:64] - with_im[64:], with_re[64:] + with_im[:64]
        straight = jnp.concatenate([scr_re, scr_im], axis=0).astype(bf16)
        turned = jnp.concatenate([scr_im, -scr_re], axis=0).astype(bf16)
        kern = (nt(wave_re[cond], straight) + nt(wave_im[cond], turned)) * (1.0 / NG)
        swapped = pltpu.roll(kern, 64, 1)
        near_re, near_im = near[128 * pair : 128 * pair + 64], near[128 * pair + 64 : 128 * pair + 128]
        direct = collect(kern * far_re + swapped * far_im, gather_hi, row_hi)
        back += swapped * near_im - kern * (near_re * minus_low)
        total += jnp.where(k == first_point[pair], jnp.broadcast_to(direct, (points, 128)), 0.0)
    back = collect(back, gather_lo, row_lo)
    total += jnp.where(k == move, jnp.broadcast_to(back, (points, 128)), 0.0)
    out_ref[...] = total


def pair_terms(place, pairs, funcs, own, other, table, held, interpret=False):
    points = held.shape[0]
    vmem, smem = pl.BlockSpec(memory_space=pltpu.VMEM), pl.BlockSpec(memory_space=pltpu.SMEM)
    return pl.pallas_call(
        pair_body,
        out_shape=jax.ShapeDtypeStruct((points, 128), jnp.float32),
        in_specs=[smem, smem] + [vmem] * 5,
        out_specs=vmem,
        scratch_shapes=[
            pltpu.VMEM((AT_ONCE * 256, 2 * PLANE), jnp.bfloat16),
            pltpu.VMEM((AT_ONCE * 256, 2 * PLANE), jnp.bfloat16),
            pltpu.VMEM((72, PLANE), jnp.float32),
            pltpu.VMEM((72, PLANE), jnp.float32),
            pltpu.VMEM((SIDE, 256, 4 * HALF), jnp.float32),
            pltpu.VMEM((256, NG), jnp.bfloat16),
            pltpu.VMEM((256, NG), jnp.bfloat16),
        ],
        compiler_params=pltpu.CompilerParams(vmem_limit_bytes=32 << 20),
        name="pair_terms",
        interpret=interpret,
    )(place, pairs, funcs, own, other, table, held)


def local(band_functions, screening, exciton, pair_list):
    bf16 = jnp.bfloat16
    points = lax.axis_size("kq")
    here, block = lax.axis_index("kq"), lax.axis_index("band")
    place = jnp.stack([here, block]).astype(jnp.int32)
    other = lax.ppermute(screening, "kq", [(i, i ^ 1) for i in range(points)])

    pieces = band_functions.reshape(2, 2, 2, 32, 128).transpose(0, 3, 1, 2, 4).reshape(points, 2, 128)
    held = lax.all_to_all(pack_pieces(pieces, exciton), "kq", 0, 0, tiled=True)

    funcs = lax.all_to_all(send_pieces(pair_list, held), ("kq", "band"), 0, 0, tiled=True)

    table = jnp.asarray(plane_table(), dtype=bf16)
    terms = pair_terms(place, pair_list, funcs, screening[0], other[0], table, held)

    rows = [[16 * y + z for z in range(16)] for y in range(8)]
    columns = [[(16 * y + z) * BLOCKS + b for y in range(8) for b in range(BLOCKS)] for z in range(16)]
    parts = lax.all_to_all(
        terms.reshape(16, 8, 128), "kq", 0, 0, tiled=True, axis_index_groups=rows
    )
    parts = jnp.sum(parts, axis=0).reshape(32, 1, 32)
    parts = lax.all_to_all(
        parts, ("kq", "band"), 0, 0, tiled=True, axis_index_groups=columns
    )
    return jnp.sum(parts, axis=(0, 1)).reshape(1, 2, 16)


def solution(mesh):
    return jax.shard_map(
        local,
        mesh=mesh,
        in_specs=(
            P("kq", None, "band", None),
            P("kq", None, None, None),
            P("kq", None, None),
            P("kq", None),
        ),
        out_specs=P("kq", None, "band"),
        check_vma=False,
    )
```

```python
import functools
import math

import jax
import jax.numpy as jnp
import numpy as np
from jax import lax
from jax.experimental import pallas as pl
from jax.experimental.pallas import tpu as pltpu
from jax.sharding import PartitionSpec as P

SIDE = 16
BOX = 8
PLANE = SIDE * SIDE
HALF = BOX * BOX
NG = BOX * HALF
BLOCKS = 4
QUARTERS = 4
AT_ONCE = 2
NT = (((1,), (1,)), ((), ()))


def plane_table():
    y, z = np.divmod(np.arange(PLANE), SIDE)
    gy, gz = np.divmod(np.arange(HALF), BOX)
    m = (y[:, None] * (gy - 4)[None] + z[:, None] * (gz - 4)[None]) % SIDE
    c, s = np.cos(2 * np.pi * m / SIDE), np.sin(2 * np.pi * m / SIDE)
    top = np.concatenate([c, -s, -s, -c], axis=1)
    low = np.concatenate([s, c, c, -s], axis=1)
    return np.concatenate([top, low], axis=0)


def weighted(terms):
    total = None
    for factor, value in terms:
        if abs(factor) < 1e-9:
            continue
        if abs(abs(factor) - 1.0) < 1e-9:
            piece = value if factor > 0 else -value
        else:
            piece = value * factor
        total = piece if total is None else total + piece
    return total


def iota(shape, axis):
    return lax.broadcasted_iota(jnp.int32, shape, axis)


def second_of(seconds_ref, block, parity):
    return seconds_ref[2 * block + parity, 1]


def pack_body(pieces_ref, exciton_ref, packed_ref):
    points = pieces_ref.shape[0]
    amps = jnp.concatenate([exciton_ref[0], jnp.zeros((2, 64), jnp.bfloat16)], axis=1)
    packed_ref[:, 0:2] = pieces_ref[...]
    packed_ref[:, 2:4] = jnp.broadcast_to(amps[None], (points, 2, 128))


def pack_pieces(pieces, exciton, interpret=False):
    points = pieces.shape[0]
    vmem = pl.BlockSpec(memory_space=pltpu.VMEM)
    return pl.pallas_call(
        pack_body,
        out_shape=jax.ShapeDtypeStruct((points, 4, 128), jnp.bfloat16),
        in_specs=[vmem, vmem],
        out_specs=vmem,
        name="pack_pieces",
        interpret=interpret,
    )(pieces, exciton)


def send_body(pairs_ref, held_ref, sent_ref, twice, built, done):
    points = held_ref.shape[0]
    part = built.shape[0] // QUARTERS
    twice[0:points] = held_ref[...]
    twice[points : 2 * points] = held_ref[...]
    moves = [[second_of(pairs_ref, block, parity) for block in range(BLOCKS)] for parity in range(2)]
    right = [[held_ref[moves[p][b], 0:2] for b in range(BLOCKS)] for p in range(2)]

    def chip(i, carry):
        for parity in range(2):
            for block in range(BLOCKS):
                target = (2 * i + parity) * BLOCKS + block
                run = 2 * i + moves[parity][block]
                built[target, 0] = twice[run + parity, 0:2]
                built[target, 1] = twice[run + (1 - parity), 0:2]
                built[target, 2] = right[parity][block]
        return carry

    copies = []
    chips = points // (2 * QUARTERS)
    for quarter in range(QUARTERS):
        lax.fori_loop(quarter * chips, (quarter + 1) * chips, chip, 0, unroll=8)
        rows = pl.ds(quarter * part, part)
        copies.append(pltpu.make_async_copy(built.at[rows], sent_ref.at[rows], done.at[quarter]))
        copies[-1].start()
    for copy in copies:
        copy.wait()


def send_pieces(pairs, held, interpret=False):
    points = held.shape[0]
    shape = (points * BLOCKS, 3, 2, 128)
    return pl.pallas_call(
        send_body,
        out_shape=jax.ShapeDtypeStruct(shape, jnp.bfloat16),
        in_specs=[
            pl.BlockSpec(memory_space=pltpu.SMEM),
            pl.BlockSpec(memory_space=pltpu.VMEM),
        ],
        out_specs=pl.BlockSpec(memory_space=pl.ANY),
        scratch_shapes=[
            pltpu.VMEM((2 * points, 4, 128), jnp.bfloat16),
            pltpu.VMEM(shape, jnp.bfloat16),
            pltpu.SemaphoreType.DMA((QUARTERS,)),
        ],
        compiler_params=pltpu.CompilerParams(vmem_limit_bytes=4 << 20),
        name="send_pieces",
        interpret=interpret,
    )(pairs, held)


def pair_body(
    place_ref,
    pairs_ref,
    funcs_ref,
    own_ref,
    other_ref,
    table_ref,
    held_ref,
    out_ref,
    dens_even,
    dens_odd,
    left_even,
    left_odd,
    sums,
    wave_re,
    wave_im,
):
    f32, bf16 = jnp.float32, jnp.bfloat16
    points = held_ref.shape[0]

    def densities(x, dens, left):
        for kind in range(2):

            def bands(ri, slot):
                parts = []
                for half in range(2):
                    piece = (ri * 32 + 2 * x + half) * 2 + kind
                    part = funcs_ref[pl.ds(piece * BLOCKS, BLOCKS), slot]
                    parts.append(part.astype(f32).reshape(8, 128))
                return jnp.concatenate(parts, axis=1)

            right_re, right_im = bands(0, 2), bands(1, 2)
            for pair in range(2):
                place = (kind * 2 + pair) * 16
                left[place : place + 8] = bands(0, pair)
                left[place + 8 : place + 16] = bands(1, pair)
                for v in range(8):
                    left_re = left[pl.ds(place + v, 8, stride=0)]
                    left_im = left[pl.ds(place + 8 + v, 8, stride=0)]
                    row = (kind * 2 + pair) * 64 + 8 * v
                    dens_re = left_re * right_re + left_im * right_im
                    dens_im = left_re * right_im - left_im * right_re
                    dens[row : row + 8, :PLANE] = dens_re.astype(bf16)
                    dens[row : row + 8, PLANE:] = dens_im.astype(bf16)

    def fill(x, dens, left):
        for i in range(AT_ONCE):
            densities(x + i, dens.at[pl.ds(256 * i, 256)], left)

    def sum_up(x, dens):
        both = jnp.dot(dens[...], table_ref[...], preferred_element_type=f32)
        for i in range(AT_ONCE):
            sums[x + i] = both[256 * i : 256 * i + 256]

    fill(0, dens_even, left_even)

    def planes(i, carry):
        x = 2 * AT_ONCE * i
        sum_up(x, dens_even)
        fill(x + AT_ONCE, dens_odd, left_odd)
        sum_up(x + AT_ONCE, dens_odd)
        fill(jnp.minimum(x + 2 * AT_ONCE, SIDE - AT_ONCE), dens_even, left_even)
        return carry

    lax.fori_loop(0, SIDE // (2 * AT_ONCE), planes, 0, unroll=2)

    scale = 1.0 / math.sqrt(SIDE**3)
    low_lanes = iota((16, 128), 1) < HALF

    def along_x(chunk, carry):
        rows = pl.ds(pl.multiple_of(chunk * 16, 16), 16)
        out = {}
        for parity in range(2):
            sign = 1.0 if parity == 0 else -1.0
            straight, turned = [], []
            for x in range(8):
                straight.append(sums[x, rows, 0:128] + sign * sums[x + 8, rows, 0:128])
                turned.append(sums[x, rows, 128:256] + sign * sums[x + 8, rows, 128:256])
            for g in (0, 2, 4) if parity == 0 else (1, 3):
                angle = [2 * math.pi * x * g / SIDE for x in range(8)]
                even = weighted([(math.cos(a), v) for a, v in zip(angle, straight)])
                odd = weighted([(math.sin(a), v) for a, v in zip(angle, turned)])
                if odd is None:
                    out[-g] = even
                else:
                    out[g], out[-g] = even + odd, even - odd
        for pair in range(4):
            first, second = out[2 * pair - 4] * scale, out[2 * pair - 3] * scale
            re = jnp.where(low_lanes, first, pltpu.roll(second, 64, 1))
            im = jnp.where(low_lanes, pltpu.roll(first, 64, 1), second)
            wave_re[rows, pair * 128 : pair * 128 + 128] = re.astype(bf16)
            wave_im[rows, pair * 128 : pair * 128 + 128] = im.astype(bf16)
        return carry

    lax.fori_loop(0, 16, along_x, 0, unroll=16)

    def nt(a, b):
        return lax.dot_general(a, b, NT, preferred_element_type=f32)

    here, block = place_ref[0], place_ref[1]
    move = second_of(pairs_ref, block, here & 1)
    first_point = [(here + move) & (points - 1), ((here ^ 1) + move) & (points - 1)]

    row, lane = iota((64, 128), 0), iota((64, 128), 1)
    row_hi, row_lo = row >> 3, row & 7
    q, l = iota((128, 128), 0), iota((128, 128), 1)
    pick_hi = jnp.where((q >> 3) == ((l >> 3) & 7), 1.0, 0.0).astype(bf16)
    pick_lo = jnp.where((q >> 3) == (l & 7), 1.0, 0.0).astype(bf16)

    def rows_of(point, row_band):
        kept = []
        for ri in range(2):
            values = jnp.broadcast_to(held_ref[point, 2 + ri : 3 + ri].astype(f32), (64, 128))
            kept.append(jnp.where((lane & 7) == row_band, values, 0.0))
        return kept

    def spread(kept, pick):
        kept = jnp.concatenate(kept, axis=0).astype(bf16)
        return jnp.dot(kept, pick, preferred_element_type=f32)

    far = spread(rows_of(move, row_lo), pick_lo)
    near = spread(rows_of(first_point[0], row_hi) + rows_of(first_point[1], row_hi), pick_hi)
    minus_low = jnp.where(lane < 64, -1.0, 1.0)
    far_re, far_im = far[:64], far[64:] * minus_low

    out_band = 2 * (l >> 5) + ((l >> 3) & 1)
    out_part = (l >> 4) & 1
    part = (q >> 6) == out_part
    gather_hi = jnp.where(part & (((q >> 3) & 7) == out_band), 1.0, 0.0).astype(bf16)
    gather_lo = jnp.where(part & ((q & 7) == out_band), 1.0, 0.0).astype(bf16)

    def collect(values, gather, row_band):
        high = values.astype(bf16)
        rest = values - high.astype(f32)
        middle = rest.astype(bf16)
        low = (rest - middle.astype(f32)).astype(bf16)
        both = sum(jnp.dot(p, gather, preferred_element_type=f32) for p in (high, middle, low))
        return jnp.sum(jnp.where(row_band == (lane & 7), both, 0.0), axis=0, keepdims=True)

    r = iota((points, 128), 0)
    k = ((r & 7) << 4) | (r >> 3)
    total = jnp.zeros((points, 128), f32)
    back = 0.0
    for pair, weights in enumerate((own_ref, other_ref)):
        val, cond = slice(64 * pair, 64 * pair + 64), slice(128 + 64 * pair, 192 + 64 * pair)
        stacked = jnp.concatenate([wave_re[val], wave_im[val]], axis=0)
        with_re, with_im = nt(stacked, weights[0]), nt(stacked, weights[1])
        scr_re, scr_im = with_re[:64] - with_im[64:], with_re[64:] + with_im[:64]
        straight = jnp.concatenate([scr_re, scr_im], axis=0).astype(bf16)
        turned = jnp.concatenate([scr_im, -scr_re], axis=0).astype(bf16)
        kern = (nt(wave_re[cond], straight) + nt(wave_im[cond], turned)) * (1.0 / NG)
        swapped = pltpu.roll(kern, 64, 1)
        near_re, near_im = near[128 * pair : 128 * pair + 64], near[128 * pair + 64 : 128 * pair + 128]
        direct = collect(kern * far_re + swapped * far_im, gather_hi, row_hi)
        back += swapped * near_im - kern * (near_re * minus_low)
        total += jnp.where(k == first_point[pair], jnp.broadcast_to(direct, (points, 128)), 0.0)
    back = collect(back, gather_lo, row_lo)
    total += jnp.where(k == move, jnp.broadcast_to(back, (points, 128)), 0.0)
    out_ref[...] = total


def pair_terms(place, pairs, funcs, own, other, table, held, interpret=False):
    points = held.shape[0]
    vmem, smem = pl.BlockSpec(memory_space=pltpu.VMEM), pl.BlockSpec(memory_space=pltpu.SMEM)
    return pl.pallas_call(
        pair_body,
        out_shape=jax.ShapeDtypeStruct((points, 128), jnp.float32),
        in_specs=[smem, smem] + [vmem] * 5,
        out_specs=vmem,
        scratch_shapes=[
            pltpu.VMEM((AT_ONCE * 256, 2 * PLANE), jnp.bfloat16),
            pltpu.VMEM((AT_ONCE * 256, 2 * PLANE), jnp.bfloat16),
            pltpu.VMEM((72, PLANE), jnp.float32),
            pltpu.VMEM((72, PLANE), jnp.float32),
            pltpu.VMEM((SIDE, 256, 4 * HALF), jnp.float32),
            pltpu.VMEM((256, NG), jnp.bfloat16),
            pltpu.VMEM((256, NG), jnp.bfloat16),
        ],
        compiler_params=pltpu.CompilerParams(vmem_limit_bytes=32 << 20),
        name="pair_terms",
        interpret=interpret,
    )(place, pairs, funcs, own, other, table, held)


def local(band_functions, screening, exciton, pair_list):
    bf16 = jnp.bfloat16
    points = lax.axis_size("kq")
    here, block = lax.axis_index("kq"), lax.axis_index("band")
    place = jnp.stack([here, block]).astype(jnp.int32)
    other = lax.ppermute(screening, "kq", [(i, i ^ 1) for i in range(points)])

    pieces = band_functions.reshape(2, 2, 2, 32, 128).transpose(0, 3, 1, 2, 4).reshape(points, 2, 128)
    held = lax.all_to_all(pack_pieces(pieces, exciton), "kq", 0, 0, tiled=True)

    funcs = lax.all_to_all(send_pieces(pair_list, held), ("kq", "band"), 0, 0, tiled=True)

    table = jnp.asarray(plane_table(), dtype=bf16)
    terms = pair_terms(place, pair_list, funcs, screening[0], other[0], table, held)

    rows = [[16 * y + z for z in range(16)] for y in range(8)]
    columns = [[(16 * y + z) * BLOCKS + b for y in range(8) for b in range(BLOCKS)] for z in range(16)]
    parts = lax.all_to_all(
        terms.reshape(16, 8, 128), "kq", 0, 0, tiled=True, axis_index_groups=rows
    )
    parts = jnp.sum(parts, axis=0).reshape(32, 1, 32)
    parts = lax.all_to_all(
        parts, ("kq", "band"), 0, 0, tiled=True, axis_index_groups=columns
    )
    return jnp.sum(parts, axis=(0, 1)).reshape(1, 2, 16)


def solution(mesh):
    return jax.shard_map(
        local,
        mesh=mesh,
        in_specs=(
            P("kq", None, "band", None),
            P("kq", None, None, None),
            P("kq", None, None),
            P("kq", None),
        ),
        out_specs=P("kq", None, "band"),
        check_vma=False,
    )
```

```python
import functools
import math

import jax
import jax.numpy as jnp
import numpy as np
from jax import lax
from jax.experimental import pallas as pl
from jax.experimental.pallas import tpu as pltpu
from jax.sharding import PartitionSpec as P

SIDE = 16
BOX = 8
PLANE = SIDE * SIDE
HALF = BOX * BOX
NG = BOX * HALF
BLOCKS = 4
QUARTERS = 4
AT_ONCE = 2
NT = (((1,), (1,)), ((), ()))


def plane_table():
    y, z = np.divmod(np.arange(PLANE), SIDE)
    gy, gz = np.divmod(np.arange(HALF), BOX)
    m = (y[:, None] * (gy - 4)[None] + z[:, None] * (gz - 4)[None]) % SIDE
    c, s = np.cos(2 * np.pi * m / SIDE), np.sin(2 * np.pi * m / SIDE)
    top = np.concatenate([c, -s, -s, -c], axis=1)
    low = np.concatenate([s, c, c, -s], axis=1)
    return np.concatenate([top, low], axis=0)


def weighted(terms):
    total = None
    for factor, value in terms:
        if abs(factor) < 1e-9:
            continue
        if abs(abs(factor) - 1.0) < 1e-9:
            piece = value if factor > 0 else -value
        else:
            piece = value * factor
        total = piece if total is None else total + piece
    return total


def iota(shape, axis):
    return lax.broadcasted_iota(jnp.int32, shape, axis)


def second_of(seconds_ref, block, parity):
    return seconds_ref[2 * block + parity, 1]


def pack_body(pieces_ref, exciton_ref, packed_ref):
    points = pieces_ref.shape[0]
    amps = jnp.concatenate([exciton_ref[0], jnp.zeros((2, 64), jnp.bfloat16)], axis=1)
    packed_ref[:, 0:2] = pieces_ref[...]
    packed_ref[:, 2:4] = jnp.broadcast_to(amps[None], (points, 2, 128))


def pack_pieces(pieces, exciton, interpret=False):
    points = pieces.shape[0]
    vmem = pl.BlockSpec(memory_space=pltpu.VMEM)
    return pl.pallas_call(
        pack_body,
        out_shape=jax.ShapeDtypeStruct((points, 4, 128), jnp.bfloat16),
        in_specs=[vmem, vmem],
        out_specs=vmem,
        name="pack_pieces",
        interpret=interpret,
    )(pieces, exciton)


def send_body(pairs_ref, held_ref, sent_ref, twice, built, done):
    points = held_ref.shape[0]
    part = built.shape[0] // QUARTERS
    twice[0:points] = held_ref[...]
    twice[points : 2 * points] = held_ref[...]
    moves = [[second_of(pairs_ref, block, parity) for block in range(BLOCKS)] for parity in range(2)]
    right = [[held_ref[moves[p][b], 0:2] for b in range(BLOCKS)] for p in range(2)]

    def chip(i, carry):
        for parity in range(2):
            for block in range(BLOCKS):
                target = (2 * i + parity) * BLOCKS + block
                run = 2 * i + moves[parity][block]
                built[target, 0] = twice[run + parity, 0:2]
                built[target, 1] = twice[run + (1 - parity), 0:2]
                built[target, 2] = right[parity][block]
        return carry

    copies = []
    chips = points // (2 * QUARTERS)
    for quarter in range(QUARTERS):
        lax.fori_loop(quarter * chips, (quarter + 1) * chips, chip, 0, unroll=8)
        rows = pl.ds(quarter * part, part)
        copies.append(pltpu.make_async_copy(built.at[rows], sent_ref.at[rows], done.at[quarter]))
        copies[-1].start()
    for copy in copies:
        copy.wait()


def send_pieces(pairs, held, interpret=False):
    points = held.shape[0]
    shape = (points * BLOCKS, 3, 2, 128)
    return pl.pallas_call(
        send_body,
        out_shape=jax.ShapeDtypeStruct(shape, jnp.bfloat16),
        in_specs=[
            pl.BlockSpec(memory_space=pltpu.SMEM),
            pl.BlockSpec(memory_space=pltpu.VMEM),
        ],
        out_specs=pl.BlockSpec(memory_space=pl.ANY),
        scratch_shapes=[
            pltpu.VMEM((2 * points, 4, 128), jnp.bfloat16),
            pltpu.VMEM(shape, jnp.bfloat16),
            pltpu.SemaphoreType.DMA((QUARTERS,)),
        ],
        compiler_params=pltpu.CompilerParams(vmem_limit_bytes=4 << 20),
        name="send_pieces",
        interpret=interpret,
    )(pairs, held)


def pair_body(
    place_ref,
    pairs_ref,
    funcs_ref,
    own_ref,
    other_ref,
    table_ref,
    held_ref,
    out_ref,
    dens_even,
    dens_odd,
    left_even,
    left_odd,
    sums,
    wave_re,
    wave_im,
):
    f32, bf16 = jnp.float32, jnp.bfloat16
    points = held_ref.shape[0]

    def densities(x, dens, left):
        for kind in range(2):

            def bands(ri, slot):
                parts = []
                for half in range(2):
                    piece = (ri * 32 + 2 * x + half) * 2 + kind
                    part = funcs_ref[pl.ds(piece * BLOCKS, BLOCKS), slot]
                    parts.append(part.astype(f32).reshape(8, 128))
                return jnp.concatenate(parts, axis=1)

            right_re, right_im = bands(0, 2), bands(1, 2)
            for pair in range(2):
                place = (kind * 2 + pair) * 16
                left[place : place + 8] = bands(0, pair)
                left[place + 8 : place + 16] = bands(1, pair)
                for v in range(8):
                    left_re = left[pl.ds(place + v, 8, stride=0)]
                    left_im = left[pl.ds(place + 8 + v, 8, stride=0)]
                    row = (kind * 2 + pair) * 64 + 8 * v
                    dens_re = left_re * right_re + left_im * right_im
                    dens_im = left_re * right_im - left_im * right_re
                    dens[row : row + 8, :PLANE] = dens_re.astype(bf16)
                    dens[row : row + 8, PLANE:] = dens_im.astype(bf16)

    def fill(x, dens, left):
        for i in range(AT_ONCE):
            densities(x + i, dens.at[pl.ds(256 * i, 256)], left)

    def sum_up(x, dens):
        both = jnp.dot(dens[...], table_ref[...], preferred_element_type=f32)
        for i in range(AT_ONCE):
            sums[x + i] = both[256 * i : 256 * i + 256]

    fill(0, dens_even, left_even)

    def planes(i, carry):
        x = 2 * AT_ONCE * i
        sum_up(x, dens_even)
        fill(x + AT_ONCE, dens_odd, left_odd)
        sum_up(x + AT_ONCE, dens_odd)
        fill(jnp.minimum(x + 2 * AT_ONCE, SIDE - AT_ONCE), dens_even, left_even)
        return carry

    lax.fori_loop(0, SIDE // (2 * AT_ONCE), planes, 0, unroll=2)

    scale = 1.0 / math.sqrt(SIDE**3)
    low_lanes = iota((16, 128), 1) < HALF

    def along_x(chunk, carry):
        rows = pl.ds(pl.multiple_of(chunk * 16, 16), 16)
        out = {}
        for parity in range(2):
            sign = 1.0 if parity == 0 else -1.0
            straight, turned = [], []
            for x in range(8):
                straight.append(sums[x, rows, 0:128] + sign * sums[x + 8, rows, 0:128])
                turned.append(sums[x, rows, 128:256] + sign * sums[x + 8, rows, 128:256])
            for g in (0, 2, 4) if parity == 0 else (1, 3):
                angle = [2 * math.pi * x * g / SIDE for x in range(8)]
                even = weighted([(math.cos(a), v) for a, v in zip(angle, straight)])
                odd = weighted([(math.sin(a), v) for a, v in zip(angle, turned)])
                if odd is None:
                    out[-g] = even
                else:
                    out[g], out[-g] = even + odd, even - odd
        for pair in range(4):
            first, second = out[2 * pair - 4] * scale, out[2 * pair - 3] * scale
            re = jnp.where(low_lanes, first, pltpu.roll(second, 64, 1))
            im = jnp.where(low_lanes, pltpu.roll(first, 64, 1), second)
            wave_re[rows, pair * 128 : pair * 128 + 128] = re.astype(bf16)
            wave_im[rows, pair * 128 : pair * 128 + 128] = im.astype(bf16)
        return carry

    lax.fori_loop(0, 16, along_x, 0, unroll=16)

    def nt(a, b):
        return lax.dot_general(a, b, NT, preferred_element_type=f32)

    here, block = place_ref[0], place_ref[1]
    move = second_of(pairs_ref, block, here & 1)
    first_point = [(here + move) & (points - 1), ((here ^ 1) + move) & (points - 1)]

    row, lane = iota((64, 128), 0), iota((64, 128), 1)
    row_hi, row_lo = row >> 3, row & 7
    q, l = iota((128, 128), 0), iota((128, 128), 1)
    pick_hi = jnp.where((q >> 3) == ((l >> 3) & 7), 1.0, 0.0).astype(bf16)
    pick_lo = jnp.where((q >> 3) == (l & 7), 1.0, 0.0).astype(bf16)

    def rows_of(point, row_band):
        kept = []
        for ri in range(2):
            values = jnp.broadcast_to(held_ref[point, 2 + ri : 3 + ri].astype(f32), (64, 128))
            kept.append(jnp.where((lane & 7) == row_band, values, 0.0))
        return kept

    def spread(kept, pick):
        kept = jnp.concatenate(kept, axis=0).astype(bf16)
        return jnp.dot(kept, pick, preferred_element_type=f32)

    far = spread(rows_of(move, row_lo), pick_lo)
    near = spread(rows_of(first_point[0], row_hi) + rows_of(first_point[1], row_hi), pick_hi)
    minus_low = jnp.where(lane < 64, -1.0, 1.0)
    far_re, far_im = far[:64], far[64:] * minus_low

    out_band = 2 * (l >> 5) + ((l >> 3) & 1)
    out_part = (l >> 4) & 1
    part = (q >> 6) == out_part
    gather_hi = jnp.where(part & (((q >> 3) & 7) == out_band), 1.0, 0.0).astype(bf16)
    gather_lo = jnp.where(part & ((q & 7) == out_band), 1.0, 0.0).astype(bf16)

    def collect(values, gather, row_band):
        high = values.astype(bf16)
        rest = values - high.astype(f32)
        middle = rest.astype(bf16)
        low = (rest - middle.astype(f32)).astype(bf16)
        both = sum(jnp.dot(p, gather, preferred_element_type=f32) for p in (high, middle, low))
        return jnp.sum(jnp.where(row_band == (lane & 7), both, 0.0), axis=0, keepdims=True)

    r = iota((points, 128), 0)
    k = ((r & 7) << 4) | (r >> 3)
    total = jnp.zeros((points, 128), f32)
    back = 0.0
    for pair, weights in enumerate((own_ref, other_ref)):
        val, cond = slice(64 * pair, 64 * pair + 64), slice(128 + 64 * pair, 192 + 64 * pair)
        stacked = jnp.concatenate([wave_re[val], wave_im[val]], axis=0)
        with_re, with_im = nt(stacked, weights[0]), nt(stacked, weights[1])
        scr_re, scr_im = with_re[:64] - with_im[64:], with_re[64:] + with_im[:64]
        straight = jnp.concatenate([scr_re, scr_im], axis=0).astype(bf16)
        turned = jnp.concatenate([scr_im, -scr_re], axis=0).astype(bf16)
        kern = (nt(wave_re[cond], straight) + nt(wave_im[cond], turned)) * (1.0 / NG)
        swapped = pltpu.roll(kern, 64, 1)
        near_re, near_im = near[128 * pair : 128 * pair + 64], near[128 * pair + 64 : 128 * pair + 128]
        direct = collect(kern * far_re + swapped * far_im, gather_hi, row_hi)
        back += swapped * near_im - kern * (near_re * minus_low)
        total += jnp.where(k == first_point[pair], jnp.broadcast_to(direct, (points, 128)), 0.0)
    back = collect(back, gather_lo, row_lo)
    total += jnp.where(k == move, jnp.broadcast_to(back, (points, 128)), 0.0)
    out_ref[...] = total.astype(out_ref.dtype)


def pair_terms(place, pairs, funcs, own, other, table, held, interpret=False):
    points = held.shape[0]
    vmem, smem = pl.BlockSpec(memory_space=pltpu.VMEM), pl.BlockSpec(memory_space=pltpu.SMEM)
    return pl.pallas_call(
        pair_body,
        out_shape=jax.ShapeDtypeStruct((points, 128), jnp.bfloat16),
        in_specs=[smem, smem] + [vmem] * 5,
        out_specs=vmem,
        scratch_shapes=[
            pltpu.VMEM((AT_ONCE * 256, 2 * PLANE), jnp.bfloat16),
            pltpu.VMEM((AT_ONCE * 256, 2 * PLANE), jnp.bfloat16),
            pltpu.VMEM((72, PLANE), jnp.float32),
            pltpu.VMEM((72, PLANE), jnp.float32),
            pltpu.VMEM((SIDE, 256, 4 * HALF), jnp.float32),
            pltpu.VMEM((256, NG), jnp.bfloat16),
            pltpu.VMEM((256, NG), jnp.bfloat16),
        ],
        compiler_params=pltpu.CompilerParams(vmem_limit_bytes=32 << 20),
        name="pair_terms",
        interpret=interpret,
    )(place, pairs, funcs, own, other, table, held)


def local(band_functions, screening, exciton, pair_list):
    bf16 = jnp.bfloat16
    points = lax.axis_size("kq")
    here, block = lax.axis_index("kq"), lax.axis_index("band")
    place = jnp.stack([here, block]).astype(jnp.int32)
    other = lax.ppermute(screening, "kq", [(i, i ^ 1) for i in range(points)])

    pieces = band_functions.reshape(2, 2, 2, 32, 128).transpose(0, 3, 1, 2, 4).reshape(points, 2, 128)
    held = lax.all_to_all(pack_pieces(pieces, exciton), "kq", 0, 0, tiled=True)

    funcs = lax.all_to_all(send_pieces(pair_list, held), ("kq", "band"), 0, 0, tiled=True)

    table = jnp.asarray(plane_table(), dtype=bf16)
    terms = pair_terms(place, pair_list, funcs, screening[0], other[0], table, held)

    rows = [[16 * y + z for z in range(16)] for y in range(8)]
    columns = [[(16 * y + z) * BLOCKS + b for y in range(8) for b in range(BLOCKS)] for z in range(16)]
    parts = lax.all_to_all(
        terms.reshape(16, 8, 128), "kq", 0, 0, tiled=True, axis_index_groups=rows
    )
    parts = jnp.sum(parts.astype(jnp.float32), axis=0).reshape(32, 1, 32)
    parts = lax.all_to_all(
        parts, ("kq", "band"), 0, 0, tiled=True, axis_index_groups=columns
    )
    return jnp.sum(parts, axis=(0, 1)).reshape(1, 2, 16)


def solution(mesh):
    return jax.shard_map(
        local,
        mesh=mesh,
        in_specs=(
            P("kq", None, "band", None),
            P("kq", None, None, None),
            P("kq", None, None),
            P("kq", None),
        ),
        out_specs=P("kq", None, "band"),
        check_vma=False,
    )
```

```python
import functools
import math

import jax
import jax.numpy as jnp
import numpy as np
from jax import lax
from jax.experimental import pallas as pl
from jax.experimental.pallas import tpu as pltpu
from jax.sharding import PartitionSpec as P

SIDE = 16
BOX = 8
PLANE = SIDE * SIDE
HALF = BOX * BOX
NG = BOX * HALF
BLOCKS = 4
QUARTERS = 4
AT_ONCE = 2
NT = (((1,), (1,)), ((), ()))


def plane_table():
    y, z = np.divmod(np.arange(PLANE), SIDE)
    gy, gz = np.divmod(np.arange(HALF), BOX)
    m = (y[:, None] * (gy - 4)[None] + z[:, None] * (gz - 4)[None]) % SIDE
    c, s = np.cos(2 * np.pi * m / SIDE), np.sin(2 * np.pi * m / SIDE)
    top = np.concatenate([c, -s, -s, -c], axis=1)
    low = np.concatenate([s, c, c, -s], axis=1)
    return np.concatenate([top, low], axis=0)


def weighted(terms):
    total = None
    for factor, value in terms:
        if abs(factor) < 1e-9:
            continue
        if abs(abs(factor) - 1.0) < 1e-9:
            piece = value if factor > 0 else -value
        else:
            piece = value * factor
        total = piece if total is None else total + piece
    return total


def iota(shape, axis):
    return lax.broadcasted_iota(jnp.int32, shape, axis)


def second_of(seconds_ref, block, parity):
    return seconds_ref[2 * block + parity, 1]


def pack_body(pieces_ref, exciton_ref, packed_ref):
    points = pieces_ref.shape[0]
    amps = jnp.concatenate([exciton_ref[0], jnp.zeros((2, 64), jnp.bfloat16)], axis=1)
    packed_ref[:, 0:2] = pieces_ref[...]
    packed_ref[:, 2:4] = jnp.broadcast_to(amps[None], (points, 2, 128))


def pack_pieces(pieces, exciton, interpret=False):
    points = pieces.shape[0]
    vmem = pl.BlockSpec(memory_space=pltpu.VMEM)
    return pl.pallas_call(
        pack_body,
        out_shape=jax.ShapeDtypeStruct((points, 4, 128), jnp.bfloat16),
        in_specs=[vmem, vmem],
        out_specs=vmem,
        name="pack_pieces",
        interpret=interpret,
    )(pieces, exciton)


def send_body(pairs_ref, held_ref, sent_ref, twice, built, done):
    points = held_ref.shape[0]
    part = built.shape[0] // QUARTERS
    twice[0:points] = held_ref[...]
    twice[points : 2 * points] = held_ref[...]
    moves = [[second_of(pairs_ref, block, parity) for block in range(BLOCKS)] for parity in range(2)]
    right = [[held_ref[moves[p][b], 0:2] for b in range(BLOCKS)] for p in range(2)]

    def chip(i, carry):
        for parity in range(2):
            for block in range(BLOCKS):
                target = (2 * i + parity) * BLOCKS + block
                run = 2 * i + moves[parity][block]
                built[target, 0] = twice[run + parity, 0:2]
                built[target, 1] = twice[run + (1 - parity), 0:2]
                built[target, 2] = right[parity][block]
        return carry

    copies = []
    chips = points // (2 * QUARTERS)
    for quarter in range(QUARTERS):
        lax.fori_loop(quarter * chips, (quarter + 1) * chips, chip, 0, unroll=8)
        rows = pl.ds(quarter * part, part)
        copies.append(pltpu.make_async_copy(built.at[rows], sent_ref.at[rows], done.at[quarter]))
        copies[-1].start()
    for copy in copies:
        copy.wait()


def send_pieces(pairs, held, interpret=False):
    points = held.shape[0]
    shape = (points * BLOCKS, 3, 2, 128)
    return pl.pallas_call(
        send_body,
        out_shape=jax.ShapeDtypeStruct(shape, jnp.bfloat16),
        in_specs=[
            pl.BlockSpec(memory_space=pltpu.SMEM),
            pl.BlockSpec(memory_space=pltpu.VMEM),
        ],
        out_specs=pl.BlockSpec(memory_space=pl.ANY),
        scratch_shapes=[
            pltpu.VMEM((2 * points, 4, 128), jnp.bfloat16),
            pltpu.VMEM(shape, jnp.bfloat16),
            pltpu.SemaphoreType.DMA((QUARTERS,)),
        ],
        compiler_params=pltpu.CompilerParams(vmem_limit_bytes=4 << 20),
        name="send_pieces",
        interpret=interpret,
    )(pairs, held)


def pair_body(
    place_ref,
    pairs_ref,
    funcs_ref,
    own_ref,
    other_ref,
    table_ref,
    held_ref,
    out_ref,
    dens_even,
    dens_odd,
    left_even,
    left_odd,
    sums,
    wave_re,
    wave_im,
):
    f32, bf16 = jnp.float32, jnp.bfloat16
    points = held_ref.shape[0]

    def densities(x, dens, left):
        for kind in range(2):

            def bands(ri, slot):
                parts = []
                for half in range(2):
                    piece = (ri * 32 + 2 * x + half) * 2 + kind
                    part = funcs_ref[pl.ds(piece * BLOCKS, BLOCKS), slot]
                    parts.append(part.astype(f32).reshape(8, 128))
                return jnp.concatenate(parts, axis=1)

            right_re, right_im = bands(0, 2), bands(1, 2)
            for pair in range(2):
                place = (kind * 2 + pair) * 16
                left[place : place + 8] = bands(0, pair)
                left[place + 8 : place + 16] = bands(1, pair)
                for v in range(8):
                    left_re = left[pl.ds(place + v, 8, stride=0)]
                    left_im = left[pl.ds(place + 8 + v, 8, stride=0)]
                    row = (kind * 2 + pair) * 64 + 8 * v
                    dens_re = left_re * right_re + left_im * right_im
                    dens_im = left_re * right_im - left_im * right_re
                    dens[row : row + 8, :PLANE] = dens_re.astype(bf16)
                    dens[row : row + 8, PLANE:] = dens_im.astype(bf16)

    def fill(x, dens, left):
        for i in range(AT_ONCE):
            densities(x + i, dens.at[pl.ds(256 * i, 256)], left)

    def sum_up(x, dens):
        both = jnp.dot(dens[...], table_ref[...], preferred_element_type=f32)
        for i in range(AT_ONCE):
            sums[x + i] = both[256 * i : 256 * i + 256]

    fill(0, dens_even, left_even)

    def planes(i, carry):
        x = 2 * AT_ONCE * i
        sum_up(x, dens_even)
        fill(x + AT_ONCE, dens_odd, left_odd)
        sum_up(x + AT_ONCE, dens_odd)
        fill(jnp.minimum(x + 2 * AT_ONCE, SIDE - AT_ONCE), dens_even, left_even)
        return carry

    lax.fori_loop(0, SIDE // (2 * AT_ONCE), planes, 0, unroll=2)

    scale = 1.0 / math.sqrt(SIDE**3)
    low_lanes = iota((16, 128), 1) < HALF

    def along_x(chunk, carry):
        rows = pl.ds(pl.multiple_of(chunk * 16, 16), 16)
        out = {}
        for parity in range(2):
            sign = 1.0 if parity == 0 else -1.0
            straight, turned = [], []
            for x in range(8):
                straight.append(sums[x, rows, 0:128] + sign * sums[x + 8, rows, 0:128])
                turned.append(sums[x, rows, 128:256] + sign * sums[x + 8, rows, 128:256])
            for g in (0, 2, 4) if parity == 0 else (1, 3):
                angle = [2 * math.pi * x * g / SIDE for x in range(8)]
                even = weighted([(math.cos(a), v) for a, v in zip(angle, straight)])
                odd = weighted([(math.sin(a), v) for a, v in zip(angle, turned)])
                if odd is None:
                    out[-g] = even
                else:
                    out[g], out[-g] = even + odd, even - odd
        for pair in range(4):
            first, second = out[2 * pair - 4] * scale, out[2 * pair - 3] * scale
            re = jnp.where(low_lanes, first, pltpu.roll(second, 64, 1))
            im = jnp.where(low_lanes, pltpu.roll(first, 64, 1), second)
            wave_re[rows, pair * 128 : pair * 128 + 128] = re.astype(bf16)
            wave_im[rows, pair * 128 : pair * 128 + 128] = im.astype(bf16)
        return carry

    lax.fori_loop(0, 16, along_x, 0, unroll=16)

    def nt(a, b):
        return lax.dot_general(a, b, NT, preferred_element_type=f32)

    here, block = place_ref[0], place_ref[1]
    move = second_of(pairs_ref, block, here & 1)
    first_point = [(here + move) & (points - 1), ((here ^ 1) + move) & (points - 1)]

    row, lane = iota((64, 128), 0), iota((64, 128), 1)
    row_hi, row_lo = row >> 3, row & 7
    q, l = iota((128, 128), 0), iota((128, 128), 1)
    pick_hi = jnp.where((q >> 3) == ((l >> 3) & 7), 1.0, 0.0).astype(bf16)
    pick_lo = jnp.where((q >> 3) == (l & 7), 1.0, 0.0).astype(bf16)

    def rows_of(point, row_band):
        kept = []
        for ri in range(2):
            values = jnp.broadcast_to(held_ref[point, 2 + ri : 3 + ri].astype(f32), (64, 128))
            kept.append(jnp.where((lane & 7) == row_band, values, 0.0))
        return kept

    def spread(kept, pick):
        kept = jnp.concatenate(kept, axis=0).astype(bf16)
        return jnp.dot(kept, pick, preferred_element_type=f32)

    far = spread(rows_of(move, row_lo), pick_lo)
    near = spread(rows_of(first_point[0], row_hi) + rows_of(first_point[1], row_hi), pick_hi)
    minus_low = jnp.where(lane < 64, -1.0, 1.0)
    far_re, far_im = far[:64], far[64:] * minus_low

    out_band = 2 * (l >> 5) + ((l >> 3) & 1)
    out_part = (l >> 4) & 1
    part = (q >> 6) == out_part
    gather_hi = jnp.where(part & (((q >> 3) & 7) == out_band), 1.0, 0.0).astype(bf16)
    gather_lo = jnp.where(part & ((q & 7) == out_band), 1.0, 0.0).astype(bf16)

    def collect(values, gather, row_band):
        high = values.astype(bf16)
        rest = values - high.astype(f32)
        middle = rest.astype(bf16)
        low = (rest - middle.astype(f32)).astype(bf16)
        both = sum(jnp.dot(p, gather, preferred_element_type=f32) for p in (high, middle, low))
        return jnp.sum(jnp.where(row_band == (lane & 7), both, 0.0), axis=0, keepdims=True)

    k = iota((points, 128), 0)
    total = jnp.zeros((points, 128), f32)
    back = 0.0
    for pair, weights in enumerate((own_ref, other_ref)):
        val, cond = slice(64 * pair, 64 * pair + 64), slice(128 + 64 * pair, 192 + 64 * pair)
        stacked = jnp.concatenate([wave_re[val], wave_im[val]], axis=0)
        with_re, with_im = nt(stacked, weights[0]), nt(stacked, weights[1])
        scr_re, scr_im = with_re[:64] - with_im[64:], with_re[64:] + with_im[:64]
        straight = jnp.concatenate([scr_re, scr_im], axis=0).astype(bf16)
        turned = jnp.concatenate([scr_im, -scr_re], axis=0).astype(bf16)
        kern = (nt(wave_re[cond], straight) + nt(wave_im[cond], turned)) * (1.0 / NG)
        swapped = pltpu.roll(kern, 64, 1)
        near_re, near_im = near[128 * pair : 128 * pair + 64], near[128 * pair + 64 : 128 * pair + 128]
        direct = collect(kern * far_re + swapped * far_im, gather_hi, row_hi)
        back += swapped * near_im - kern * (near_re * minus_low)
        total += jnp.where(k == first_point[pair], jnp.broadcast_to(direct, (points, 128)), 0.0)
    back = collect(back, gather_lo, row_lo)
    total += jnp.where(k == move, jnp.broadcast_to(back, (points, 128)), 0.0)
    out_ref[...] = total


def pair_terms(place, pairs, funcs, own, other, table, held, interpret=False):
    points = held.shape[0]
    vmem, smem = pl.BlockSpec(memory_space=pltpu.VMEM), pl.BlockSpec(memory_space=pltpu.SMEM)
    return pl.pallas_call(
        pair_body,
        out_shape=jax.ShapeDtypeStruct((points, 128), jnp.float32),
        in_specs=[smem, smem] + [vmem] * 5,
        out_specs=vmem,
        scratch_shapes=[
            pltpu.VMEM((AT_ONCE * 256, 2 * PLANE), jnp.bfloat16),
            pltpu.VMEM((AT_ONCE * 256, 2 * PLANE), jnp.bfloat16),
            pltpu.VMEM((72, PLANE), jnp.float32),
            pltpu.VMEM((72, PLANE), jnp.float32),
            pltpu.VMEM((SIDE, 256, 4 * HALF), jnp.float32),
            pltpu.VMEM((256, NG), jnp.bfloat16),
            pltpu.VMEM((256, NG), jnp.bfloat16),
        ],
        compiler_params=pltpu.CompilerParams(vmem_limit_bytes=32 << 20),
        name="pair_terms",
        interpret=interpret,
    )(place, pairs, funcs, own, other, table, held)


def local(band_functions, screening, exciton, pair_list):
    bf16 = jnp.bfloat16
    points = lax.axis_size("kq")
    here, block = lax.axis_index("kq"), lax.axis_index("band")
    place = jnp.stack([here, block]).astype(jnp.int32)
    other = lax.ppermute(screening, "kq", [(i, i ^ 1) for i in range(points)])

    pieces = band_functions.reshape(2, 2, 2, 32, 128).transpose(0, 3, 1, 2, 4).reshape(points, 2, 128)
    held = lax.all_to_all(pack_pieces(pieces, exciton), "kq", 0, 0, tiled=True)

    funcs = lax.all_to_all(send_pieces(pair_list, held), ("kq", "band"), 0, 0, tiled=True)

    table = jnp.asarray(plane_table(), dtype=bf16)
    terms = pair_terms(place, pair_list, funcs, screening[0], other[0], table, held)

    parts = lax.all_to_all(terms.reshape(points, 1, 128), "kq", 0, 0, tiled=True)
    parts = jnp.sum(parts, axis=0).reshape(BLOCKS, 1, 32)
    parts = lax.all_to_all(parts, "band", 0, 0, tiled=True)
    return jnp.sum(parts, axis=(0, 1)).reshape(1, 2, 16)


def solution(mesh):
    return jax.shard_map(
        local,
        mesh=mesh,
        in_specs=(
            P("kq", None, "band", None),
            P("kq", None, None, None),
            P("kq", None, None),
            P("kq", None),
        ),
        out_specs=P("kq", None, "band"),
        check_vma=False,
    )
```

```python
import functools
import math

import jax
import jax.numpy as jnp
import numpy as np
from jax import lax
from jax.experimental import pallas as pl
from jax.experimental.pallas import tpu as pltpu
from jax.sharding import PartitionSpec as P

SIDE = 16
BOX = 8
PLANE = SIDE * SIDE
HALF = BOX * BOX
NG = BOX * HALF
BLOCKS = 4
QUARTERS = 4
AT_ONCE = 2
NT = (((1,), (1,)), ((), ()))


def plane_table():
    y, z = np.divmod(np.arange(PLANE), SIDE)
    gy, gz = np.divmod(np.arange(HALF), BOX)
    m = (y[:, None] * (gy - 4)[None] + z[:, None] * (gz - 4)[None]) % SIDE
    c, s = np.cos(2 * np.pi * m / SIDE), np.sin(2 * np.pi * m / SIDE)
    top = np.concatenate([c, -s, -s, -c], axis=1)
    low = np.concatenate([s, c, c, -s], axis=1)
    return np.concatenate([top, low], axis=0)


def weighted(terms):
    total = None
    for factor, value in terms:
        if abs(factor) < 1e-9:
            continue
        if abs(abs(factor) - 1.0) < 1e-9:
            piece = value if factor > 0 else -value
        else:
            piece = value * factor
        total = piece if total is None else total + piece
    return total


def iota(shape, axis):
    return lax.broadcasted_iota(jnp.int32, shape, axis)


def second_of(seconds_ref, block, parity):
    return seconds_ref[2 * block + parity, 1]


def pack_body(pieces_ref, exciton_ref, packed_ref, arrived, built, came, went):
    half = built.shape[0] // 2
    rows = [pl.ds(0, half), pl.ds(half, half)]
    incoming = [
        pltpu.make_async_copy(pieces_ref.at[rows[h]], arrived.at[rows[h]], came.at[h]) for h in range(2)
    ]
    outgoing = [
        pltpu.make_async_copy(built.at[rows[h]], packed_ref.at[rows[h]], went.at[h]) for h in range(2)
    ]
    for copy in incoming:
        copy.start()
    amps = jnp.concatenate([exciton_ref[0], jnp.zeros((2, 64), jnp.bfloat16)], axis=1)
    for h in range(2):
        built[rows[h], 2:4] = jnp.broadcast_to(amps[None], (half, 2, 128))
        incoming[h].wait()
        built[rows[h], 0:2] = arrived[rows[h]]
        outgoing[h].start()
    for copy in outgoing:
        copy.wait()


def pack_pieces(pieces, exciton, interpret=False):
    points = pieces.shape[0]
    return pl.pallas_call(
        pack_body,
        out_shape=jax.ShapeDtypeStruct((points, 4, 128), jnp.bfloat16),
        in_specs=[pl.BlockSpec(memory_space=pl.ANY), pl.BlockSpec(memory_space=pltpu.VMEM)],
        out_specs=pl.BlockSpec(memory_space=pl.ANY),
        scratch_shapes=[
            pltpu.VMEM((points, 2, 128), jnp.bfloat16),
            pltpu.VMEM((points, 4, 128), jnp.bfloat16),
            pltpu.SemaphoreType.DMA((2,)),
            pltpu.SemaphoreType.DMA((2,)),
        ],
        name="pack_pieces",
        interpret=interpret,
    )(pieces, exciton)


def send_body(pairs_ref, held_ref, sent_ref, twice, built, done):
    points = held_ref.shape[0]
    part = built.shape[0] // QUARTERS
    twice[0:points] = held_ref[...]
    twice[points : 2 * points] = held_ref[...]
    moves = [[second_of(pairs_ref, block, parity) for block in range(BLOCKS)] for parity in range(2)]
    right = [[held_ref[moves[p][b], 0:2] for b in range(BLOCKS)] for p in range(2)]

    def chip(i, carry):
        for parity in range(2):
            for block in range(BLOCKS):
                target = (2 * i + parity) * BLOCKS + block
                run = 2 * i + moves[parity][block]
                built[target, 0] = twice[run + parity, 0:2]
                built[target, 1] = twice[run + (1 - parity), 0:2]
                built[target, 2] = right[parity][block]
        return carry

    copies = []
    chips = points // (2 * QUARTERS)
    for quarter in range(QUARTERS):
        lax.fori_loop(quarter * chips, (quarter + 1) * chips, chip, 0, unroll=8)
        rows = pl.ds(quarter * part, part)
        copies.append(pltpu.make_async_copy(built.at[rows], sent_ref.at[rows], done.at[quarter]))
        copies[-1].start()
    for copy in copies:
        copy.wait()


def send_pieces(pairs, held, interpret=False):
    points = held.shape[0]
    shape = (points * BLOCKS, 3, 2, 128)
    return pl.pallas_call(
        send_body,
        out_shape=jax.ShapeDtypeStruct(shape, jnp.bfloat16),
        in_specs=[
            pl.BlockSpec(memory_space=pltpu.SMEM),
            pl.BlockSpec(memory_space=pltpu.VMEM),
        ],
        out_specs=pl.BlockSpec(memory_space=pl.ANY),
        scratch_shapes=[
            pltpu.VMEM((2 * points, 4, 128), jnp.bfloat16),
            pltpu.VMEM(shape, jnp.bfloat16),
            pltpu.SemaphoreType.DMA((QUARTERS,)),
        ],
        compiler_params=pltpu.CompilerParams(vmem_limit_bytes=4 << 20),
        name="send_pieces",
        interpret=interpret,
    )(pairs, held)


def pair_body(
    place_ref,
    pairs_ref,
    funcs_ref,
    own_ref,
    other_ref,
    table_ref,
    held_ref,
    out_ref,
    dens_even,
    dens_odd,
    left_even,
    left_odd,
    sums,
    wave_re,
    wave_im,
):
    f32, bf16 = jnp.float32, jnp.bfloat16
    points = held_ref.shape[0]

    def densities(x, dens, left):
        for kind in range(2):

            def bands(ri, slot):
                parts = []
                for half in range(2):
                    piece = (ri * 32 + 2 * x + half) * 2 + kind
                    part = funcs_ref[pl.ds(piece * BLOCKS, BLOCKS), slot]
                    parts.append(part.astype(f32).reshape(8, 128))
                return jnp.concatenate(parts, axis=1)

            right_re, right_im = bands(0, 2), bands(1, 2)
            for pair in range(2):
                place = (kind * 2 + pair) * 16
                left[place : place + 8] = bands(0, pair)
                left[place + 8 : place + 16] = bands(1, pair)
                for v in range(8):
                    left_re = left[pl.ds(place + v, 8, stride=0)]
                    left_im = left[pl.ds(place + 8 + v, 8, stride=0)]
                    row = (kind * 2 + pair) * 64 + 8 * v
                    dens_re = left_re * right_re + left_im * right_im
                    dens_im = left_re * right_im - left_im * right_re
                    dens[row : row + 8, :PLANE] = dens_re.astype(bf16)
                    dens[row : row + 8, PLANE:] = dens_im.astype(bf16)

    def fill(x, dens, left):
        for i in range(AT_ONCE):
            densities(x + i, dens.at[pl.ds(256 * i, 256)], left)

    def sum_up(x, dens):
        both = jnp.dot(dens[...], table_ref[...], preferred_element_type=f32)
        for i in range(AT_ONCE):
            sums[x + i] = both[256 * i : 256 * i + 256]

    fill(0, dens_even, left_even)

    def planes(i, carry):
        x = 2 * AT_ONCE * i
        sum_up(x, dens_even)
        fill(x + AT_ONCE, dens_odd, left_odd)
        sum_up(x + AT_ONCE, dens_odd)
        fill(jnp.minimum(x + 2 * AT_ONCE, SIDE - AT_ONCE), dens_even, left_even)
        return carry

    lax.fori_loop(0, SIDE // (2 * AT_ONCE), planes, 0, unroll=2)

    scale = 1.0 / math.sqrt(SIDE**3)
    low_lanes = iota((16, 128), 1) < HALF

    def along_x(chunk, carry):
        rows = pl.ds(pl.multiple_of(chunk * 16, 16), 16)
        out = {}
        for parity in range(2):
            sign = 1.0 if parity == 0 else -1.0
            straight, turned = [], []
            for x in range(8):
                straight.append(sums[x, rows, 0:128] + sign * sums[x + 8, rows, 0:128])
                turned.append(sums[x, rows, 128:256] + sign * sums[x + 8, rows, 128:256])
            for g in (0, 2, 4) if parity == 0 else (1, 3):
                angle = [2 * math.pi * x * g / SIDE for x in range(8)]
                even = weighted([(math.cos(a), v) for a, v in zip(angle, straight)])
                odd = weighted([(math.sin(a), v) for a, v in zip(angle, turned)])
                if odd is None:
                    out[-g] = even
                else:
                    out[g], out[-g] = even + odd, even - odd
        for pair in range(4):
            first, second = out[2 * pair - 4] * scale, out[2 * pair - 3] * scale
            re = jnp.where(low_lanes, first, pltpu.roll(second, 64, 1))
            im = jnp.where(low_lanes, pltpu.roll(first, 64, 1), second)
            wave_re[rows, pair * 128 : pair * 128 + 128] = re.astype(bf16)
            wave_im[rows, pair * 128 : pair * 128 + 128] = im.astype(bf16)
        return carry

    lax.fori_loop(0, 16, along_x, 0, unroll=16)

    def nt(a, b):
        return lax.dot_general(a, b, NT, preferred_element_type=f32)

    here, block = place_ref[0], place_ref[1]
    move = second_of(pairs_ref, block, here & 1)
    first_point = [(here + move) & (points - 1), ((here ^ 1) + move) & (points - 1)]

    row, lane = iota((64, 128), 0), iota((64, 128), 1)
    row_hi, row_lo = row >> 3, row & 7
    q, l = iota((128, 128), 0), iota((128, 128), 1)
    pick_hi = jnp.where((q >> 3) == ((l >> 3) & 7), 1.0, 0.0).astype(bf16)
    pick_lo = jnp.where((q >> 3) == (l & 7), 1.0, 0.0).astype(bf16)

    def rows_of(point, row_band):
        kept = []
        for ri in range(2):
            values = jnp.broadcast_to(held_ref[point, 2 + ri : 3 + ri].astype(f32), (64, 128))
            kept.append(jnp.where((lane & 7) == row_band, values, 0.0))
        return kept

    def spread(kept, pick):
        kept = jnp.concatenate(kept, axis=0).astype(bf16)
        return jnp.dot(kept, pick, preferred_element_type=f32)

    far = spread(rows_of(move, row_lo), pick_lo)
    near = spread(rows_of(first_point[0], row_hi) + rows_of(first_point[1], row_hi), pick_hi)
    minus_low = jnp.where(lane < 64, -1.0, 1.0)
    far_re, far_im = far[:64], far[64:] * minus_low

    out_band = 2 * (l >> 5) + ((l >> 3) & 1)
    out_part = (l >> 4) & 1
    part = (q >> 6) == out_part
    gather_hi = jnp.where(part & (((q >> 3) & 7) == out_band), 1.0, 0.0).astype(bf16)
    gather_lo = jnp.where(part & ((q & 7) == out_band), 1.0, 0.0).astype(bf16)

    def collect(values, gather, row_band):
        high = values.astype(bf16)
        rest = values - high.astype(f32)
        middle = rest.astype(bf16)
        low = (rest - middle.astype(f32)).astype(bf16)
        both = sum(jnp.dot(p, gather, preferred_element_type=f32) for p in (high, middle, low))
        return jnp.sum(jnp.where(row_band == (lane & 7), both, 0.0), axis=0, keepdims=True)

    r = iota((points, 128), 0)
    k = ((r & 7) << 4) | (r >> 3)
    total = jnp.zeros((points, 128), f32)
    back = 0.0
    for pair, weights in enumerate((own_ref, other_ref)):
        val, cond = slice(64 * pair, 64 * pair + 64), slice(128 + 64 * pair, 192 + 64 * pair)
        stacked = jnp.concatenate([wave_re[val], wave_im[val]], axis=0)
        with_re, with_im = nt(stacked, weights[0]), nt(stacked, weights[1])
        scr_re, scr_im = with_re[:64] - with_im[64:], with_re[64:] + with_im[:64]
        straight = jnp.concatenate([scr_re, scr_im], axis=0).astype(bf16)
        turned = jnp.concatenate([scr_im, -scr_re], axis=0).astype(bf16)
        kern = (nt(wave_re[cond], straight) + nt(wave_im[cond], turned)) * (1.0 / NG)
        swapped = pltpu.roll(kern, 64, 1)
        near_re, near_im = near[128 * pair : 128 * pair + 64], near[128 * pair + 64 : 128 * pair + 128]
        direct = collect(kern * far_re + swapped * far_im, gather_hi, row_hi)
        back += swapped * near_im - kern * (near_re * minus_low)
        total += jnp.where(k == first_point[pair], jnp.broadcast_to(direct, (points, 128)), 0.0)
    back = collect(back, gather_lo, row_lo)
    total += jnp.where(k == move, jnp.broadcast_to(back, (points, 128)), 0.0)
    out_ref[...] = total.astype(out_ref.dtype)


def pair_terms(place, pairs, funcs, own, other, table, held, interpret=False):
    points = held.shape[0]
    vmem, smem = pl.BlockSpec(memory_space=pltpu.VMEM), pl.BlockSpec(memory_space=pltpu.SMEM)
    return pl.pallas_call(
        pair_body,
        out_shape=jax.ShapeDtypeStruct((points, 128), jnp.bfloat16),
        in_specs=[smem, smem] + [vmem] * 5,
        out_specs=vmem,
        scratch_shapes=[
            pltpu.VMEM((AT_ONCE * 256, 2 * PLANE), jnp.bfloat16),
            pltpu.VMEM((AT_ONCE * 256, 2 * PLANE), jnp.bfloat16),
            pltpu.VMEM((72, PLANE), jnp.float32),
            pltpu.VMEM((72, PLANE), jnp.float32),
            pltpu.VMEM((SIDE, 256, 4 * HALF), jnp.float32),
            pltpu.VMEM((256, NG), jnp.bfloat16),
            pltpu.VMEM((256, NG), jnp.bfloat16),
        ],
        compiler_params=pltpu.CompilerParams(vmem_limit_bytes=32 << 20),
        name="pair_terms",
        interpret=interpret,
    )(place, pairs, funcs, own, other, table, held)


def local(band_functions, screening, exciton, pair_list):
    bf16 = jnp.bfloat16
    points = lax.axis_size("kq")
    here, block = lax.axis_index("kq"), lax.axis_index("band")
    place = jnp.stack([here, block]).astype(jnp.int32)
    other = lax.ppermute(screening, "kq", [(i, i ^ 1) for i in range(points)])

    pieces = band_functions.reshape(2, 2, 2, 32, 128).transpose(0, 3, 1, 2, 4).reshape(points, 2, 128)
    held = lax.all_to_all(pack_pieces(pieces, exciton), "kq", 0, 0, tiled=True)

    funcs = lax.all_to_all(send_pieces(pair_list, held), ("kq", "band"), 0, 0, tiled=True)

    table = jnp.asarray(plane_table(), dtype=bf16)
    terms = pair_terms(place, pair_list, funcs, screening[0], other[0], table, held)

    rows = [[16 * y + z for z in range(16)] for y in range(8)]
    columns = [[(16 * y + z) * BLOCKS + b for y in range(8) for b in range(BLOCKS)] for z in range(16)]
    parts = lax.all_to_all(
        terms.reshape(16, 8, 128), "kq", 0, 0, tiled=True, axis_index_groups=rows
    )
    parts = jnp.sum(parts.astype(jnp.float32), axis=0).reshape(32, 1, 32)
    parts = lax.all_to_all(
        parts, ("kq", "band"), 0, 0, tiled=True, axis_index_groups=columns
    )
    return jnp.sum(parts, axis=(0, 1)).reshape(1, 2, 16)


def solution(mesh):
    return jax.shard_map(
        local,
        mesh=mesh,
        in_specs=(
            P("kq", None, "band", None),
            P("kq", None, None, None),
            P("kq", None, None),
            P("kq", None),
        ),
        out_specs=P("kq", None, "band"),
        check_vma=False,
    )
```
